256 devices in a mesh: work: 32 (over y, x, core), tile: 8 (over z).
Axes of the slice: x: 4, y: 4, z: 8, core: 2. Of those that a mesh axis runs over, the one named last changes fastest.
Arguments:
- block_coords: float32 [32768, 3, 128], P(('work', 'tile')), may hold values from -6 to 6
- block_visibilities: float32 [32768, 4, 128], P(('work', 'tile')), may hold values from -6 to 6
- subgrid_of_block: int32 [32768], P(('work', 'tile')), may hold values from 0 to 511, as said below
- live_blocks: int32 [256], P(('work', 'tile')), may hold values from 96 to 128, as said below
- corners: int32 [512, 2], replicated, may hold values from 0 to 4064, as said below
- channel_scale: float32 [2], replicated, may hold values from 0.85 to 1.15
Outputs:
- uv_grid: float32 [4, 512, 4096], P(None, 'tile', 'work')
The draws below stay inside these ranges and needn't reach their ends.
Inputs may be any that keep to these rules, and one draw needn't show every extreme that they name: `subgrid_of_block`: subgrid s belongs to the strip of worker s // 16. Among the 128 blocks of one device at most 16 belong to subgrids of one worker, and some worker gets exactly 16 blocks from every device. Device d in the order of the axes work, tile holds the blocks d * 128 to (d + 1) * 128 - 1; its first live_blocks[d] blocks are live, the others take no part. Some device has all its blocks live. Subgrid s covers rows corners[s, 0] to corners[s, 0] + 31 of the window, and columns corners[s, 1] to corners[s, 1] + 31, all inside columns 128 (s // 16) to 128 (s // 16 + 1) - 1.
All inputs are finite; a program needn't handle non-finite values.
Results may differ from the reference program's by a relative error of at most 0.0003.
Values sent between devices are 32-bit elements; how exact they have to be, the bound alone decides.
No kernel may reach another device: no remote copies, remote signals or barrier semaphores. Data moves between devices by JAX's collectives and lax.ppermute only.
A program may use at most 192 MiB of HBM per device.

```python
import math
import jax
import jax.numpy as jnp
from jax import lax

CH = 2
SUB = 32
ROWS = 128
BLK_DEV = 128
GCW = 128
SUBW = 16
MAX_DEVICE_BLOCKS = 16
SOURCES = 256
STRIPS_PER_WORKER = 32
BLOCKS = 32768
NSUB = 512
GR = 512
GC = 4096


def route_workers(key):
    busiest_worker = jax.random.randint(jax.random.fold_in(key, 11), (), 0, STRIPS_PER_WORKER)
    crowd_penalty = jax.random.randint(jax.random.fold_in(key, 12), (STRIPS_PER_WORKER,), 0, 4) * 4096
    worker_index = jnp.arange(STRIPS_PER_WORKER, dtype=jnp.int32)
    further_credit = crowd_penalty + jnp.where(worker_index == busiest_worker, 1 << 20, 0)
    local_position = jnp.arange(MAX_DEVICE_BLOCKS, dtype=jnp.int32)
    boundary_worker = (worker_index[:, None] == 0) | (worker_index[:, None] == STRIPS_PER_WORKER - 1)
    added_credit = jnp.where(boundary_worker & (local_position[None, :] == 0), 1 << 19, 0)
    position_index = jnp.arange(STRIPS_PER_WORKER * MAX_DEVICE_BLOCKS, dtype=jnp.int32).reshape(STRIPS_PER_WORKER, MAX_DEVICE_BLOCKS)

    def one_source(source_key):
        starting_score = jax.random.randint(source_key, (STRIPS_PER_WORKER, MAX_DEVICE_BLOCKS), 0, 16384)
        scores_by_worker = (starting_score + further_credit[:, None] + added_credit) * (STRIPS_PER_WORKER * MAX_DEVICE_BLOCKS) + position_index
        chosen = lax.top_k(scores_by_worker.reshape(-1), BLK_DEV)[1]
        owners = chosen // MAX_DEVICE_BLOCKS
        slots = chosen % MAX_DEVICE_BLOCKS
        order = jax.random.permutation(jax.random.fold_in(source_key, 5), BLK_DEV)
        return (owners[order], slots[order])
    source_keys = jax.random.split(jax.random.fold_in(key, 13), SOURCES)
    return jax.vmap(one_source)(source_keys)


def draw_subgrid_of_block(key, part):
    owners, slots = route_workers(key)
    within = jax.random.randint(jax.random.fold_in(key, 14), owners.shape, 0, SUBW)
    within = jnp.where((owners == STRIPS_PER_WORKER - 1) & (slots == 0), SUBW - 1, within)
    within = jnp.where((owners == 0) & (slots == 0), 0, within)
    return (owners * SUBW + within).reshape(-1).astype(jnp.int32)


def draw_live_blocks(key, part):
    counts = jax.random.randint(key, (SOURCES,), BLK_DEV - BLK_DEV // 4, BLK_DEV + 1)
    fullest = jax.random.randint(jax.random.fold_in(key, 21), (), 0, SOURCES)
    sparsest = (fullest + 1) % SOURCES
    source_ids = jnp.arange(SOURCES, dtype=jnp.int32)
    counts = jnp.where(source_ids == sparsest, BLK_DEV - BLK_DEV // 4, counts)
    counts = jnp.where(source_ids == fullest, BLK_DEV, counts)
    return counts.astype(jnp.int32)


def draw_corners(key, part):
    row_first = jax.random.randint(jax.random.fold_in(key, 31), (NSUB,), 0, GR - SUB + 1)
    col_offset = jax.random.randint(jax.random.fold_in(key, 32), (NSUB,), 0, GCW - SUB + 1)
    edge_cols = jax.random.randint(jax.random.fold_in(key, 33), (STRIPS_PER_WORKER,), 0, SUBW)
    edge_rows = jax.random.randint(jax.random.fold_in(key, 34), (STRIPS_PER_WORKER,), 0, SUBW)
    subgrid_ids = jnp.arange(NSUB, dtype=jnp.int32)
    within = subgrid_ids % SUBW
    strip = subgrid_ids // SUBW
    col_offset = jnp.where(within == edge_cols[strip], GCW - SUB, col_offset)
    row_first = jnp.where(within == edge_rows[strip], GR - SUB, row_first)
    row_first = jnp.where(within == (edge_rows[strip] + 1) % SUBW, 0, row_first)
    return jnp.stack([row_first, strip * GCW + col_offset], axis=1).astype(jnp.int32)


def block_levels(rng, shape, cuts, least, largest):
    level, own = 1.0, jax.random.fold_in(rng, 6)
    for axis_at, blocks in cuts:
        draws = jnp.exp(jax.random.uniform(jax.random.fold_in(own, axis_at), (blocks,), jnp.float32, least / len(cuts), largest / len(cuts)))
        level = level * jnp.repeat(draws, shape[axis_at] // blocks).reshape([-1 if axis == axis_at else 1 for axis in range(len(shape))])
    return level


def centred(rng, dims, scale, most, cuts=(), kind=jnp.bfloat16):
    loudness = block_levels(rng, dims, cuts, -0.22, 0.18) if cuts else 1.0
    array = jax.random.normal(rng, dims, jnp.float32) * scale * loudness
    return jnp.minimum(jnp.maximum(array, -most), most).astype(kind)


def setup_inputs(seed: int = 0) -> dict:
    seeds = jax.random.split(jax.random.key(seed), 7)
    return {
        "block_coords": jnp.clip(jax.random.uniform(seeds[0], (BLOCKS, 3, ROWS), jnp.float32, -6.0, 6.0) * block_levels(seeds[0], (BLOCKS, 3, ROWS), ((0, 256),), -0.4, 0.0), -6.0, 6.0),
        "block_visibilities": centred(seeds[1], (BLOCKS, 2 * CH, ROWS), 1.0, 6.0, ((0, 256),), jnp.float32),
        "subgrid_of_block": draw_subgrid_of_block(jax.random.fold_in(seeds[6], 71), 0),
        "live_blocks": draw_live_blocks(jax.random.fold_in(seeds[6], 71), 0),
        "corners": draw_corners(jax.random.fold_in(seeds[6], 71), 0),
        "channel_scale": jnp.clip(jax.random.uniform(seeds[5], (CH,), jnp.float32, 0.85, 1.15), 0.85, 1.15),
    }


two_pi = 2.0 * math.pi
highest = lax.Precision.HIGHEST


def pixel_offsets():
    return (jnp.arange(SUB, dtype=jnp.float32) - SUB // 2) / SUB


def block_pictures(coords, waves, channel_scale):
    offsets = pixel_offsets()
    squares = offsets * offsets
    layers = []
    for channel in range(CH):
        factor = channel_scale[channel]
        first_coord = coords[:, 0, :] * factor
        second_coord = coords[:, 1, :] * factor
        depth_coord = coords[:, 2, :] * factor
        depth_term = depth_coord[:, None, :] * squares[None, :, None]
        phase_first = two_pi * (first_coord[:, None, :] * offsets[None, :, None] + depth_term)
        phase_second = two_pi * (second_coord[:, None, :] * offsets[None, :, None] + depth_term)
        wave_real = waves[:, 2 * channel, :][:, None, :]
        wave_imag = waves[:, 2 * channel + 1, :][:, None, :]
        cosine_first = jnp.cos(phase_first)
        sine_first = jnp.sin(phase_first)
        cosine_second = jnp.cos(phase_second)
        sine_second = jnp.sin(phase_second)
        left_side = jnp.concatenate([wave_real * cosine_first - wave_imag * sine_first, wave_real * sine_first + wave_imag * cosine_first], axis=2)
        right_real = jnp.concatenate([cosine_second, -sine_second], axis=2)
        right_imag = jnp.concatenate([sine_second, cosine_second], axis=2)
        right_side = jnp.concatenate([right_real, right_imag], axis=1)
        layers.append(jnp.einsum("nxk,njk->nxj", left_side, right_side, precision=highest))
    return jnp.stack(layers, axis=1)


def transform_matrix():
    offsets = jnp.arange(SUB, dtype=jnp.int32)
    taper_values = jnp.sin(jnp.pi * (offsets.astype(jnp.float32) + 0.5) / SUB) ** 2
    product = (offsets[:, None] * offsets[None, :]) % SUB
    angles = two_pi * product.astype(jnp.float32) / SUB
    real_part = taper_values[:, None] * jnp.cos(angles)
    imag_part = -taper_values[:, None] * jnp.sin(angles)
    upper = jnp.concatenate([real_part, imag_part], axis=1)
    lower = jnp.concatenate([-imag_part, real_part], axis=1)
    return jnp.concatenate([upper, lower], axis=0)


def to_spectrum(pictures):
    amount = pictures.shape[0]
    matrix = transform_matrix()
    first = jnp.einsum("ncxj,jq->ncxq", pictures, matrix, precision=highest)
    first = first.reshape(amount, CH, SUB, 2, SUB)
    second = jnp.einsum("ncxpl,pxqk->ncqkl", first, matrix.reshape(2, SUB, 2, SUB), precision=highest)
    return (second * (1.0 / (ROWS * SUB))).reshape(amount, 2 * CH, SUB, SUB)


def place(canvas, spectra, row_start, col_start):
    offsets = jnp.arange(SUB, dtype=jnp.int32)
    row_index = row_start[:, None, None, None] + offsets[None, None, :, None]
    col_index = col_start[:, None, None, None] + offsets[None, None, None, :]
    layer_index = jnp.arange(2 * CH, dtype=jnp.int32)[None, :, None, None]
    height = canvas.shape[1]
    inside = (row_index >= 0) & (row_index < height)
    row_index = jnp.where(inside, row_index, height)
    return canvas.at[layer_index, row_index, col_index].add(spectra, mode="drop")


def reference(block_coords, block_visibilities, subgrid_of_block, live_blocks, corners, channel_scale):
    sources = live_blocks.shape[0]
    per_source = block_coords.shape[0] // sources
    coords_split = block_coords.reshape(sources, per_source, 3, ROWS)
    waves_split = block_visibilities.reshape(sources, per_source, 2 * CH, ROWS)
    labels_split = subgrid_of_block.reshape(sources, per_source)
    position = jnp.arange(per_source, dtype=jnp.int32)

    def accumulate(totals, inputs):
        coords_part, waves_part, labels_part, live_count = inputs
        live_mask = (position < live_count).astype(jnp.float32)
        pictures = block_pictures(coords_part, waves_part * live_mask[:, None, None], channel_scale)
        return totals.at[labels_part].add(pictures), None

    start = jnp.zeros((NSUB, CH, SUB, 2 * SUB), jnp.float32)
    totals = lax.scan(accumulate, start, (coords_split, waves_split, labels_split, live_blocks))[0]
    spectra = to_spectrum(totals)
    canvas = jnp.zeros((2 * CH, GR, GC), jnp.float32)
    return place(canvas, spectra, corners[:, 0], corners[:, 1])
```

```python
import functools
import math

import jax
import jax.numpy as jnp
import numpy as np
from jax import lax
from jax.experimental import pallas as pl
from jax.experimental.pallas import tpu as pltpu
from jax.sharding import PartitionSpec as P

CH = 2
SUB = 32
HALF = SUB // 2
ROWS = 128
TR = 64
GCW = 128
SUBW = 16
FIELDS = 3 + 2 * CH
TERMS = 4 * HALF

NT = (((1,), (1,)), ((), ()))


def pack_kernel(label_ref, live_ref, coords_ref, waves_ref, out_ref, count_ref):
    workers, capacity = out_ref.shape[0], SUBW
    out_ref[...] = jnp.zeros_like(out_ref)

    def clear(worker, carry):
        count_ref[worker] = 0
        return carry

    lax.fori_loop(0, workers, clear, 0)
    lane = lax.broadcasted_iota(jnp.int32, (1, ROWS), 1)

    def move(block, carry):
        label = label_ref[block]
        worker = label // SUBW
        slot = count_ref[worker]
        count_ref[worker] = slot + 1
        for field in range(3):
            out_ref[worker, pl.ds(field * capacity + slot, 1), :] = coords_ref[
                field, pl.ds(block, 1), :
            ]
        for field in range(2 * CH):
            out_ref[worker, pl.ds((3 + field) * capacity + slot, 1), :] = waves_ref[
                block, pl.ds(field, 1), :
            ]
        row = pl.ds(FIELDS * capacity, 1)
        inside = (label - worker * SUBW).astype(jnp.float32)
        out_ref[worker, row, :] = jnp.where(lane == slot, inside, out_ref[worker, row, :])
        return carry

    lax.fori_loop(0, live_ref[0], move, 0)


def pack(labels, live, coords, waves, workers):
    smem = pl.BlockSpec(memory_space=pltpu.SMEM)
    vmem = pl.BlockSpec(memory_space=pltpu.VMEM)
    return pl.pallas_call(
        pack_kernel,
        name="pack",
        out_shape=jax.ShapeDtypeStruct((workers, FIELDS * SUBW + 8, ROWS), jnp.float32),
        in_specs=[smem, smem, vmem, vmem],
        out_specs=vmem,
        scratch_shapes=[pltpu.SMEM((workers,), jnp.int32)],
    )(labels, live, coords, waves)


def sin_cos(theta, sin_terms, cos_terms):
    square = theta * theta
    sine = jnp.full_like(theta, (-1.0) ** (sin_terms - 1) / math.factorial(2 * sin_terms - 1))
    for n in range(sin_terms - 2, -1, -1):
        sine = sine * square + (-1.0) ** n / math.factorial(2 * n + 1)
    cosine = jnp.full_like(theta, (-1.0) ** (cos_terms - 1) / math.factorial(2 * cos_terms - 2))
    for n in range(cos_terms - 2, -1, -1):
        cosine = cosine * square + (-1.0) ** n / math.factorial(2 * n)
    return cosine, sine * theta


def times(a, b):
    return a[0] * b[0] - a[1] * b[1], a[0] * b[1] + a[1] * b[0]


def split(value):
    high = value.astype(jnp.bfloat16)
    low = (value - high.astype(jnp.float32)).astype(jnp.bfloat16)
    return high, low


def picture_kernel(
    label_ref, scale_ref, corner_ref, x_ref, mix_ref, spread_ref, out_ref, sums, left, right, strip
):
    step = pl.program_id(0)
    capacity = SUBW

    @pl.when(step == 0)
    def _():
        sums[...] = jnp.zeros_like(sums)
        strip[...] = jnp.zeros_like(strip)

    def field(index):
        return x_ref[0, index * capacity : (index + 1) * capacity, :]

    u, v, w = field(0), field(1), field(2)
    for ch in range(CH):
        factor = scale_ref[ch]
        first = u * factor * (2.0 * math.pi / (2 * SUB))
        second = v * factor * (2.0 * math.pi / (2 * SUB))
        depth = w * factor * (2.0 * math.pi / (SUB * SUB))
        along_u = sin_cos(first - depth * 0.5, 5, 6)
        along_v = sin_cos(second - depth * 0.5, 5, 6)
        turn = sin_cos(depth * 2.0, 4, 4)
        start = sin_cos(depth - (first + second), 7, 8)
        step_u = times(along_u, along_u)
        step_v = times(along_v, along_v)
        wave = times((field(3 + 2 * ch), field(4 + 2 * ch)), start)
        chirp = turn
        grown = turn
        for k in range(HALF):
            if k > 1:
                grown = times(grown, turn)
                chirp = times(chirp, grown)
            if k > 0:
                along_u = times(along_u, step_u)
                along_v = times(along_v, step_v)
            scaled = times(wave, chirp) if k > 0 else wave

            def put(ref, kind, value):
                ref[ch, pl.ds((kind * HALF + k) * capacity, capacity), :] = value

            put(left, 0, scaled[0] * along_u[0])
            put(left, 1, scaled[1] * along_u[0])
            put(left, 2, scaled[0] * along_u[1])
            put(left, 3, scaled[1] * along_u[1])
            if k > 0:
                put(right, 0, chirp[0] * along_v[0])
                put(right, 1, chirp[1] * along_v[0])
                put(right, 2, chirp[0] * along_v[1])
                put(right, 3, chirp[1] * along_v[1])
            else:
                put(right, 0, along_v[0])
                put(right, 1, jnp.zeros_like(u))
                put(right, 2, along_v[1])
                put(right, 3, jnp.zeros_like(u))
    for slot in range(capacity):
        label = label_ref[step * capacity + slot]
        for ch in range(CH):
            left_high, left_low = split(left[ch, pl.ds(slot, TERMS, stride=capacity), :])
            right_high, right_low = split(right[ch, pl.ds(slot, TERMS, stride=capacity), :])
            sums[label, ch] += lax.dot_general(
                jnp.concatenate([left_high, left_high, left_low], axis=1),
                jnp.concatenate([right_high, right_low, right_high], axis=1),
                NT,
                preferred_element_type=jnp.float32,
            )

    @pl.when(step == pl.num_programs(0) - 1)
    def _():
        for subgrid in range(SUBW):
            shift = corner_ref[subgrid, 1]
            spread_real = pltpu.roll(spread_ref[0], shift, 1)
            spread_imag = pltpu.roll(spread_ref[1], shift, 1)
            spread = jnp.concatenate([spread_real, spread_imag], axis=1)
            for ch in range(CH):
                wide = jnp.dot(
                    sums[subgrid, ch],
                    spread,
                    precision=lax.Precision.HIGHEST,
                    preferred_element_type=jnp.float32,
                )
                spectrum = jnp.dot(
                    mix_ref[...],
                    jnp.concatenate([wide[:, :GCW], wide[:, GCW:]], axis=0),
                    precision=lax.Precision.HIGHEST,
                    preferred_element_type=jnp.float32,
                )
                rows = pl.ds(corner_ref[subgrid, 0], SUB)
                strip[2 * ch, rows, :] += spectrum[:SUB]
                strip[2 * ch + 1, rows, :] += spectrum[SUB:]
        for tile in range(out_ref.shape[0]):
            for plane in range(2 * CH):
                out_ref[tile, plane] = strip[plane, tile * TR : (tile + 1) * TR, :]


def transform_tables():
    k = np.arange(SUB)[:, None]
    h = np.arange(HALF)[None, :]

    def tapered(x):
        return np.sin(np.pi * (x + 0.5) / SUB) ** 2 * np.exp(-2j * np.pi * k * x / SUB)

    upper, lower = tapered(HALF + h), tapered(HALF - 1 - h)
    even, odd = upper + lower, upper - lower
    table = np.concatenate([even, 1j * even, 1j * odd, -odd], axis=1)
    real, imag = table.real, table.imag
    mix = np.concatenate(
        [np.concatenate([real, -imag], axis=1), np.concatenate([imag, real], axis=1)], axis=0
    ) / (ROWS * SUB)
    spread = np.zeros((2, TERMS, GCW))
    spread[0, :, :SUB] = real.T
    spread[1, :, :SUB] = imag.T
    return mix.astype(np.float32), spread.astype(np.float32)


def picture_strip(labels, scale, corners, arrived, tiles):
    sources = arrived.shape[0]
    mix, spread = transform_tables()
    return pl.pallas_call(
        picture_kernel,
        name="pictures",
        out_shape=jax.ShapeDtypeStruct((tiles, 2 * CH, TR, GCW), jnp.float32),
        grid_spec=pltpu.PrefetchScalarGridSpec(
            num_scalar_prefetch=3,
            grid=(sources,),
            in_specs=[
                pl.BlockSpec((1, arrived.shape[1], ROWS), lambda i, *_: (i, 0, 0)),
                pl.BlockSpec(mix.shape, lambda i, *_: (0, 0)),
                pl.BlockSpec(spread.shape, lambda i, *_: (0, 0, 0)),
            ],
            out_specs=pl.BlockSpec((tiles, 2 * CH, TR, GCW), lambda i, *_: (0, 0, 0, 0)),
            scratch_shapes=[
                pltpu.VMEM((SUBW, CH, TERMS, TERMS), jnp.float32),
                pltpu.VMEM((CH, TERMS * SUBW, ROWS), jnp.float32),
                pltpu.VMEM((CH, TERMS * SUBW, ROWS), jnp.float32),
                pltpu.VMEM((2 * CH, TR * tiles, GCW), jnp.float32),
            ],
        ),
        compiler_params=pltpu.CompilerParams(dimension_semantics=("arbitrary",)),
    )(labels, scale, corners, arrived, jnp.asarray(mix), jnp.asarray(spread))


def local(block_coords, block_visibilities, subgrid_of_block, live_blocks, corners, channel_scale):
    workers = lax.axis_size("work")
    tiles = lax.axis_size("tile")
    worker = lax.axis_index("work")
    coords = jnp.swapaxes(block_coords, 0, 1)
    packed = pack(subgrid_of_block, live_blocks, coords, block_visibilities, workers)
    arrived = lax.all_to_all(packed, "work", split_axis=0, concat_axis=0, tiled=True)
    labels = arrived[:, FIELDS * SUBW, :SUBW].astype(jnp.int32).reshape(workers * SUBW)
    local_corners = lax.dynamic_slice_in_dim(corners, worker * SUBW, SUBW, 0)
    local_corners = local_corners - jnp.stack([0 * worker, worker * GCW])[None, :]
    strip = picture_strip(labels, channel_scale, local_corners, arrived, tiles)
    gathered = lax.all_to_all(strip, "tile", split_axis=0, concat_axis=0, tiled=True)
    return gathered.sum(axis=0)


def solution(mesh):
    return jax.shard_map(
        local,
        mesh=mesh,
        in_specs=(
            P(("work", "tile"), None, None),
            P(("work", "tile"), None, None),
            P(("work", "tile")),
            P(("work", "tile")),
            P(),
            P(),
        ),
        out_specs=P(None, "tile", "work"),
        check_vma=False,
    )
```

```python
import functools
import math

import jax
import jax.numpy as jnp
import numpy as np
from jax import lax
from jax.experimental import pallas as pl
from jax.experimental.pallas import tpu as pltpu
from jax.sharding import PartitionSpec as P

CH = 2
SUB = 32
HALF = SUB // 2
ROWS = 128
TR = 64
GCW = 128
SUBW = 16
FIELDS = 3 + 2 * CH
TERMS = 4 * HALF
GROUP = 8
UNROLL = 8

def pack_kernel(label_ref, live_ref, coords_ref, waves_ref, out_ref, count_ref):
    workers, capacity = out_ref.shape[0], SUBW
    out_ref[...] = jnp.zeros_like(out_ref)

    def clear(worker, carry):
        count_ref[worker] = 0
        return carry

    lax.fori_loop(0, workers, clear, 0)
    lane = lax.broadcasted_iota(jnp.int32, (1, ROWS), 1)

    live = live_ref[0]

    def move(group, carry):
        for offset in range(UNROLL):
            block = group * UNROLL + offset
            label = label_ref[block]
            worker = label // SUBW
            slot = count_ref[worker]
            count_ref[worker] = slot + 1
            kept = jnp.where(block < live, 1.0, 0.0)
            for field in range(3):
                out_ref[worker, pl.ds(field * capacity + slot, 1), :] = coords_ref[
                    field, pl.ds(block, 1), :
                ]
            for field in range(2 * CH):
                out_ref[worker, pl.ds((3 + field) * capacity + slot, 1), :] = (
                    waves_ref[block, pl.ds(field, 1), :] * kept
                )
            row = pl.ds(FIELDS * capacity, 1)
            inside = (label - worker * SUBW).astype(jnp.float32)
            out_ref[worker, row, :] = jnp.where(lane == slot, inside, out_ref[worker, row, :])
        return carry

    lax.fori_loop(0, label_ref.shape[0] // UNROLL, move, 0)


def pack(labels, live, coords, waves, workers):
    smem = pl.BlockSpec(memory_space=pltpu.SMEM)
    vmem = pl.BlockSpec(memory_space=pltpu.VMEM)
    return pl.pallas_call(
        pack_kernel,
        name="pack",
        out_shape=jax.ShapeDtypeStruct((workers, FIELDS * SUBW + 8, ROWS), jnp.float32),
        in_specs=[smem, smem, vmem, vmem],
        out_specs=vmem,
        scratch_shapes=[pltpu.SMEM((workers,), jnp.int32)],
    )(labels, live, coords, waves)


def series(square, first, count):
    terms = [(-1.0) ** n / math.factorial(2 * n + first) for n in range(count)]
    total = square * terms[-1] + terms[-2]
    for term in terms[-3::-1]:
        total = total * square + term
    return total


def sin_cos(theta, sin_terms, cos_terms):
    square = theta * theta
    return series(square, 0, cos_terms), series(square, 1, sin_terms) * theta


def times(a, b):
    return a[0] * b[0] - a[1] * b[1], a[0] * b[1] + a[1] * b[0]


def split(value):
    high = value.astype(jnp.bfloat16)
    low = (value - high.astype(jnp.float32)).astype(jnp.bfloat16)
    return high, low


def advance(current, previous, twice_sine):
    return (
        previous[0] - twice_sine * current[1],
        previous[1] + twice_sine * current[0],
    )


def factor_rows(fields, factor, put_left, put_right):
    u, v, w = fields[:3]
    first = u * (factor * (2.0 * math.pi / (2 * SUB)))
    second = v * (factor * (2.0 * math.pi / (2 * SUB)))
    depth = w * (factor * (math.pi / (SUB * SUB)))
    along_u = sin_cos(first - depth, 5, 5)
    along_v = sin_cos(second - depth, 5, 5)
    turn = sin_cos(depth * 4.0, 3, 3)
    twice_u = along_u[0] * along_u[1] * 4.0
    twice_v = along_v[0] * along_v[1] * 4.0
    twice_w = turn[1] * 2.0
    both = times(along_u, along_v)
    wave = times(fields[3:], (both[0], -both[1]))
    before_u = (along_u[0], -along_u[1])
    before_v = (along_v[0], -along_v[1])
    zero = jnp.zeros_like(u)
    chirp = before_grown = (jnp.ones_like(u), zero)
    grown = turn
    for k in range(HALF):
        if k > 0:
            if k > 1:
                grown, before_grown = advance(grown, before_grown, twice_w), grown
                chirp = times(chirp, grown)
            else:
                chirp = turn
            wave = times(wave, grown)
            along_u, before_u = advance(along_u, before_u, twice_u), along_u
            along_v, before_v = advance(along_v, before_v, twice_v), along_v
        put_left(0, k, wave[0] * along_u[0])
        put_left(1, k, wave[1] * along_u[0])
        put_left(2, k, wave[0] * along_u[1])
        put_left(3, k, wave[1] * along_u[1])
        put_right(0, k, chirp[0] * along_v[0] if k > 0 else along_v[0])
        put_right(1, k, chirp[1] * along_v[0] if k > 0 else zero)
        put_right(2, k, chirp[0] * along_v[1] if k > 0 else along_v[1])
        put_right(3, k, chirp[1] * along_v[1] if k > 0 else zero)


def product(left, right, contract):
    left_high, left_low = split(left)
    right_high, right_low = split(right)
    return lax.dot_general(
        jnp.concatenate([left_high, left_high, left_low], axis=1),
        jnp.concatenate([right_high, right_low, right_high], axis=contract),
        (((1,), (contract,)), ((), ())),
        preferred_element_type=jnp.float32,
    )


def picture_kernel(
    label_ref,
    scale_ref,
    corner_ref,
    tile_ref,
    x_ref,
    mix_ref,
    spread_ref,
    out_ref,
    left,
    right,
    strip,
    *sums,
):
    step = pl.program_id(0)
    capacity = SUBW
    tiles = out_ref.shape[0]

    @pl.when(step == 0)
    def _():
        for ch in range(CH):
            sums[ch][...] = jnp.zeros_like(sums[ch])
        strip[...] = jnp.zeros_like(strip)

    def factors(group, ch):
        def field(index):
            start = index * capacity + group * GROUP
            return x_ref[0, start : start + GROUP, :]

        def put(ref, kind, k, value):
            ref[ch, group, pl.ds((kind * HALF + k) * GROUP, GROUP), :] = value

        chosen = [field(index) for index in (0, 1, 2, 3 + 2 * ch, 4 + 2 * ch)]
        factor_rows(
            chosen, scale_ref[ch], functools.partial(put, left), functools.partial(put, right)
        )

    def gather(group, ch):
        for slot in range(GROUP):
            label = label_ref[step * capacity + group * GROUP + slot]
            rows = pl.ds(slot, TERMS, stride=GROUP)
            sums[ch][label] += product(left[ch, group, rows, :], right[ch, group, rows, :], 1)

    units = [(group, ch) for group in range(capacity // GROUP) for ch in range(CH)]
    factors(*units[0])
    for unit, following in zip(units[:-1], units[1:]):
        factors(*following)
        gather(*unit)
    gather(*units[-1])

    @pl.when(step == pl.num_programs(0) - 1)
    def _():
        for subgrid in range(SUBW):
            shift = corner_ref[subgrid, 1]
            spread_real = pltpu.roll(spread_ref[0], shift, 1)
            spread_imag = pltpu.roll(spread_ref[1], shift, 1)
            spread = jnp.concatenate([spread_real, spread_imag], axis=1)
            rows = pl.ds(corner_ref[subgrid, 0], SUB)
            for ch in range(CH):
                wide = product(sums[ch][subgrid], spread, 0)
                stacked = jnp.concatenate([wide[:, :GCW], wide[:, GCW:]], axis=0)
                spectrum = product(mix_ref[...], stacked, 0)
                strip[2 * ch, rows, :] += spectrum[:SUB]
                strip[2 * ch + 1, rows, :] += spectrum[SUB:]
        for distance in range(tiles):
            tile = lax.rem(tile_ref[0] + distance, tiles)
            for plane in range(2 * CH):
                out_ref[distance, plane] = strip[
                    plane, pl.ds(pl.multiple_of(tile * TR, TR), TR), :
                ]


def transform_tables():
    k = np.arange(SUB)[:, None]
    h = np.arange(HALF)[None, :]

    def tapered(x):
        return np.sin(np.pi * (x + 0.5) / SUB) ** 2 * np.exp(-2j * np.pi * k * x / SUB)

    upper, lower = tapered(HALF + h), tapered(HALF - 1 - h)
    even, odd = upper + lower, upper - lower
    table = np.concatenate([even, 1j * even, 1j * odd, -odd], axis=1)
    real, imag = table.real, table.imag
    mix = np.concatenate(
        [np.concatenate([real, -imag], axis=1), np.concatenate([imag, real], axis=1)], axis=0
    ) / (ROWS * SUB)
    spread = np.zeros((2, TERMS, GCW))
    spread[0, :, :SUB] = real.T
    spread[1, :, :SUB] = imag.T
    return mix.astype(np.float32), spread.astype(np.float32)


def picture_strip(labels, scale, corners, tile, arrived, tiles):
    sources = arrived.shape[0]
    mix, spread = transform_tables()
    return pl.pallas_call(
        picture_kernel,
        name="pictures",
        out_shape=jax.ShapeDtypeStruct((tiles, 2 * CH, TR, GCW), jnp.float32),
        grid_spec=pltpu.PrefetchScalarGridSpec(
            num_scalar_prefetch=4,
            grid=(sources,),
            in_specs=[
                pl.BlockSpec((1, arrived.shape[1], ROWS), lambda i, *_: (i, 0, 0)),
                pl.BlockSpec(mix.shape, lambda i, *_: (0, 0)),
                pl.BlockSpec(spread.shape, lambda i, *_: (0, 0, 0)),
            ],
            out_specs=pl.BlockSpec((tiles, 2 * CH, TR, GCW), lambda i, *_: (0, 0, 0, 0)),
            scratch_shapes=[
                pltpu.VMEM((CH, SUBW // GROUP, TERMS * GROUP, ROWS), jnp.float32),
                pltpu.VMEM((CH, SUBW // GROUP, TERMS * GROUP, ROWS), jnp.float32),
                pltpu.VMEM((2 * CH, TR * tiles, GCW), jnp.float32),
            ]
            + [pltpu.VMEM((SUBW, TERMS, TERMS), jnp.float32)] * CH,
        ),
        compiler_params=pltpu.CompilerParams(dimension_semantics=("arbitrary",)),
    )(labels, scale, corners, tile, arrived, jnp.asarray(mix), jnp.asarray(spread))


def summed_around(parts, axis):
    size = lax.axis_size(axis)
    far = size // 2
    up = [(i, (i + 1) % size) for i in range(size)]
    down = [(i, (i - 1) % size) for i in range(size)]
    rising = lax.ppermute(parts[far, :CH], axis, up)
    falling = lax.ppermute(parts[far, CH:], axis, down)
    for distance in range(far - 1, 0, -1):
        near, opposite = parts[distance], parts[size - distance]
        if distance == far - 1:
            rising = jnp.concatenate([near[:CH] + rising, near[CH:]])
            falling = jnp.concatenate([opposite[:CH], opposite[CH:] + falling])
        else:
            rising, falling = near + rising, opposite + falling
        rising = lax.ppermute(rising, axis, up)
        falling = lax.ppermute(falling, axis, down)
    return parts[0] + rising + falling


def local(block_coords, block_visibilities, subgrid_of_block, live_blocks, corners, channel_scale):
    workers = lax.axis_size("work")
    tiles = lax.axis_size("tile")
    worker = lax.axis_index("work")
    coords = jnp.swapaxes(block_coords, 0, 1)
    packed = pack(subgrid_of_block, live_blocks, coords, block_visibilities, workers)
    arrived = lax.all_to_all(packed, "work", split_axis=0, concat_axis=0, tiled=True)
    labels = arrived[:, FIELDS * SUBW, :SUBW].astype(jnp.int32).reshape(workers * SUBW)
    local_corners = lax.dynamic_slice_in_dim(corners, worker * SUBW, SUBW, 0)
    local_corners = local_corners - jnp.stack([0 * worker, worker * GCW])[None, :]
    tile = lax.axis_index("tile").astype(jnp.int32).reshape(1)
    parts = picture_strip(labels, channel_scale, local_corners, tile, arrived, tiles)
    return summed_around(parts, "tile")


def solution(mesh):
    return jax.shard_map(
        local,
        mesh=mesh,
        in_specs=(
            P(("work", "tile"), None, None),
            P(("work", "tile"), None, None),
            P(("work", "tile")),
            P(("work", "tile")),
            P(),
            P(),
        ),
        out_specs=P(None, "tile", "work"),
        check_vma=False,
    )
```

```python
import functools
import math

import jax
import jax.numpy as jnp
import numpy as np
from jax import lax
from jax.experimental import pallas as pl
from jax.experimental.pallas import tpu as pltpu
from jax.sharding import PartitionSpec as P

CH = 2
SUB = 32
HALF = SUB // 2
ROWS = 128
TR = 64
GCW = 128
SUBW = 16
FIELDS = 3 + 2 * CH
TERMS = 4 * HALF
GROUP = 8
SPAN = 2
UNROLL = 8

def pack_kernel(label_ref, live_ref, coords_ref, waves_ref, out_ref, count_ref):
    workers, capacity = out_ref.shape[0], SUBW
    out_ref[...] = jnp.zeros_like(out_ref)

    def clear(worker, carry):
        count_ref[worker] = 0
        return carry

    lax.fori_loop(0, workers, clear, 0)
    lane = lax.broadcasted_iota(jnp.int32, (1, ROWS), 1)

    live = live_ref[0]

    def move(group, carry):
        for offset in range(UNROLL):
            block = group * UNROLL + offset
            label = label_ref[block]
            worker = label // SUBW
            slot = count_ref[worker]
            count_ref[worker] = slot + 1
            kept = jnp.where(block < live, 1.0, 0.0)
            for field in range(3):
                out_ref[worker, pl.ds(field * capacity + slot, 1), :] = coords_ref[
                    field, pl.ds(block, 1), :
                ]
            for field in range(2 * CH):
                out_ref[worker, pl.ds((3 + field) * capacity + slot, 1), :] = (
                    waves_ref[block, pl.ds(field, 1), :] * kept
                )
            row = pl.ds(FIELDS * capacity, 1)
            inside = (label - worker * SUBW).astype(jnp.float32)
            out_ref[worker, row, :] = jnp.where(lane == slot, inside, out_ref[worker, row, :])
        return carry

    lax.fori_loop(0, label_ref.shape[0] // UNROLL, move, 0)


def pack(labels, live, coords, waves, workers):
    smem = pl.BlockSpec(memory_space=pltpu.SMEM)
    vmem = pl.BlockSpec(memory_space=pltpu.VMEM)
    return pl.pallas_call(
        pack_kernel,
        name="pack",
        out_shape=jax.ShapeDtypeStruct((workers, FIELDS * SUBW + 8, ROWS), jnp.float32),
        in_specs=[smem, smem, vmem, vmem],
        out_specs=vmem,
        scratch_shapes=[pltpu.SMEM((workers,), jnp.int32)],
        compiler_params=pltpu.CompilerParams(vmem_limit_bytes=8 << 20),
    )(labels, live, coords, waves)


def series(square, first, count):
    terms = [(-1.0) ** n / math.factorial(2 * n + first) for n in range(count)]
    total = square * terms[-1] + terms[-2]
    for term in terms[-3::-1]:
        total = total * square + term
    return total


def sin_cos(theta, sin_terms, cos_terms):
    square = theta * theta
    return series(square, 0, cos_terms), series(square, 1, sin_terms) * theta


def times(a, b):
    return a[0] * b[0] - a[1] * b[1], a[0] * b[1] + a[1] * b[0]


def split(value):
    high = value.astype(jnp.bfloat16)
    low = (value - high.astype(jnp.float32)).astype(jnp.bfloat16)
    return high, low


def advance(current, previous, twice_sine):
    return (
        previous[0] - twice_sine * current[1],
        previous[1] + twice_sine * current[0],
    )


def exchange(value):
    return pltpu.roll(value, GROUP // 2, 0)


def interleave(even, odd, low):
    return (
        jnp.where(low, even, exchange(odd)),
        jnp.where(low, exchange(even), odd),
    )


def interleave_pair(even, odd, low):
    real, imag = interleave(even[0], odd[0], low), interleave(even[1], odd[1], low)
    return (real[0], imag[0]), (real[1], imag[1])


def factor_rows(fields, factor, low, put_left, put_right):
    u, v, w = fields[:3]
    first = u * (factor * (2.0 * math.pi / (2 * SUB)))
    second = v * (factor * (2.0 * math.pi / (2 * SUB)))
    depth = w * (factor * (math.pi / (SUB * SUB)))
    along_u = sin_cos(first - depth, 5, 5)
    along_v = sin_cos(second - depth, 5, 5)
    turn = sin_cos(depth * 4.0, 3, 3)
    whole_u, whole_v = times(along_u, along_u), times(along_v, along_v)
    turn2 = times(turn, turn)
    turn3 = times(turn2, turn)
    both = times(along_u, along_v)
    wave = times(fields[3:], (both[0], -both[1]))
    one, zero = jnp.ones_like(u), jnp.zeros_like(u)
    all_u = interleave_pair(along_u, times(whole_u, along_u), low)
    all_v = interleave_pair(along_v, times(whole_v, along_v), low)
    all_wave = interleave_pair(wave, times(wave, turn), low)
    all_chirp = interleave_pair((one, zero), turn, low)
    all_grown = interleave_pair(turn3, times(turn3, turn2), low)
    all_before = interleave_pair((turn[0], -turn[1]), turn, low)
    twice_u = interleave(*[whole_u[0] * whole_u[1] * 4.0] * 2, low)
    twice_v = interleave(*[whole_v[0] * whole_v[1] * 4.0] * 2, low)
    twice_w = interleave(*[turn2[0] * turn2[1] * 4.0] * 2, low)
    for half in range(2):
        along_u, along_v = all_u[half], all_v[half]
        wave, chirp = all_wave[half], all_chirp[half]
        grown, before_grown = all_grown[half], all_before[half]
        before_u = (exchange(along_u[0]), -exchange(along_u[1]))
        before_v = (exchange(along_v[0]), -exchange(along_v[1]))
        for k in range(HALF // 2):
            if k > 0:
                chirp = times(chirp, grown)
                wave = times(wave, grown)
                along_u, before_u = advance(along_u, before_u, twice_u[half]), along_u
                along_v, before_v = advance(along_v, before_v, twice_v[half]), along_v
                grown, before_grown = advance(grown, before_grown, twice_w[half]), grown
            put_left(half, 0, k, wave[0] * along_u[0])
            put_left(half, 1, k, wave[1] * along_u[0])
            put_left(half, 2, k, wave[0] * along_u[1])
            put_left(half, 3, k, wave[1] * along_u[1])
            put_right(half, 0, k, chirp[0] * along_v[0])
            put_right(half, 1, k, chirp[1] * along_v[0])
            put_right(half, 2, k, chirp[0] * along_v[1])
            put_right(half, 3, k, chirp[1] * along_v[1])


def product(left, right, contract):
    left_high, left_low = split(left)
    right_high, right_low = split(right)
    return lax.dot_general(
        jnp.concatenate([left_high, left_high, left_low], axis=1),
        jnp.concatenate([right_high, right_low, right_high], axis=contract),
        (((1,), (contract,)), ((), ())),
        preferred_element_type=jnp.float32,
    )


def picture_kernel(
    ch,
    label_ref,
    scale_ref,
    corner_ref,
    x_ref,
    mix_ref,
    spread_ref,
    out_ref,
    left,
    right,
    sums,
    mixed,
    wide,
    strip,
):
    step = pl.program_id(0)
    capacity = SUBW
    tiles = out_ref.shape[0]
    part = GROUP // 2

    @pl.when(step == 0)
    def _():
        sums[...] = jnp.zeros_like(sums)

    low = lax.broadcasted_iota(jnp.int32, (GROUP, ROWS), 0) < part
    units = [
        (source, group) for source in range(x_ref.shape[0]) for group in range(capacity // GROUP)
    ]

    def factors(unit):
        source, group = units[unit]

        def field(index):
            start = index * capacity + group * GROUP
            return x_ref[source, start : start + GROUP, :]

        def put(ref, half, kind, k, value):
            ref[unit, half, pl.ds(kind * HALF * part + k * GROUP, GROUP), :] = value

        chosen = [field(index) for index in (0, 1, 2, 3 + 2 * ch, 4 + 2 * ch)]
        factor_rows(
            chosen, scale_ref[ch], low, functools.partial(put, left), functools.partial(put, right)
        )

    def gather(unit):
        for slot in range(GROUP):
            label = label_ref[(step * len(units) + unit) * GROUP + slot]
            rows = pl.ds(slot % part, TERMS, stride=part)
            half = slot // part
            sums[label] += product(left[unit, half, rows, :], right[unit, half, rows, :], 1)

    factors(0)
    for unit in range(1, len(units)):
        factors(unit)
        gather(unit - 1)
    gather(len(units) - 1)

    @pl.when(step == pl.num_programs(0) - 1)
    def _():
        strip[...] = jnp.zeros_like(strip)
        for subgrid in range(SUBW):
            mixed[subgrid * 2 * SUB : (subgrid + 1) * 2 * SUB, :] = product(
                mix_ref[...], sums[subgrid], 0
            )
        wide[...] = product(mixed[...], spread_ref[...], 0)
        for subgrid in range(SUBW):
            shift = corner_ref[subgrid, 1]
            rows = pl.ds(corner_ref[subgrid, 0], SUB)
            top = pl.ds(subgrid * 2 * SUB, SUB)
            bottom = pl.ds(subgrid * 2 * SUB + SUB, SUB)
            real = wide[top, :GCW] - wide[bottom, GCW:]
            imag = wide[top, GCW:] + wide[bottom, :GCW]
            strip[0, rows, :] += pltpu.roll(real, shift, 1)
            strip[1, rows, :] += pltpu.roll(imag, shift, 1)
        for tile in range(tiles):
            for plane in range(2):
                out_ref[tile, plane] = strip[plane, tile * TR : (tile + 1) * TR, :]


def transform_tables():
    k = np.arange(SUB)[:, None]
    h = np.arange(HALF)[None, :]

    def tapered(x):
        return np.sin(np.pi * (x + 0.5) / SUB) ** 2 * np.exp(-2j * np.pi * k * x / SUB)

    upper, lower = tapered(HALF + h), tapered(HALF - 1 - h)
    even, odd = upper + lower, upper - lower
    table = np.concatenate([even, 1j * even, 1j * odd, -odd], axis=1)
    real, imag = table.real, table.imag
    mix = np.concatenate([real, imag], axis=0) / (ROWS * SUB)
    spread = np.zeros((TERMS, 2 * GCW))
    spread[:, :SUB] = real.T
    spread[:, GCW : GCW + SUB] = imag.T
    return mix.astype(np.float32), spread.astype(np.float32)


def channel_strip(ch, labels, scale, corners, arrived, tiles):
    sources = arrived.shape[0]
    mix, spread = transform_tables()
    parts = (SPAN * SUBW // GROUP, 2, TERMS * GROUP // 2, ROWS)
    return pl.pallas_call(
        functools.partial(picture_kernel, ch),
        name="pictures",
        out_shape=jax.ShapeDtypeStruct((tiles, 2, TR, GCW), jnp.float32),
        grid_spec=pltpu.PrefetchScalarGridSpec(
            num_scalar_prefetch=3,
            grid=(sources // SPAN,),
            in_specs=[
                pl.BlockSpec((SPAN, arrived.shape[1], ROWS), lambda i, *_: (i, 0, 0)),
                pl.BlockSpec(mix.shape, lambda i, *_: (0, 0)),
                pl.BlockSpec(spread.shape, lambda i, *_: (0, 0)),
            ],
            out_specs=pl.BlockSpec((tiles, 2, TR, GCW), lambda i, *_: (0, 0, 0, 0)),
            scratch_shapes=[
                pltpu.VMEM(parts, jnp.float32),
                pltpu.VMEM(parts, jnp.float32),
                pltpu.VMEM((SUBW, TERMS, TERMS), jnp.float32),
                pltpu.VMEM((SUBW * 2 * SUB, TERMS), jnp.float32),
                pltpu.VMEM((SUBW * 2 * SUB, 2 * GCW), jnp.float32),
                pltpu.VMEM((2, TR * tiles, GCW), jnp.float32),
            ],
        ),
        compiler_params=pltpu.CompilerParams(
            dimension_semantics=("arbitrary",), vmem_limit_bytes=20 << 20
        ),
        cost_estimate=pl.CostEstimate(
            flops=3 * 2 * sources * SUBW * TERMS * TERMS * ROWS,
            bytes_accessed=4 * (arrived.size + tiles * 2 * TR * GCW),
            transcendentals=0,
        ),
    )(labels, scale, corners, arrived, jnp.asarray(mix), jnp.asarray(spread))


def local(block_coords, block_visibilities, subgrid_of_block, live_blocks, corners, channel_scale):
    workers = lax.axis_size("work")
    tiles = lax.axis_size("tile")
    worker = lax.axis_index("work")
    coords = jnp.swapaxes(block_coords, 0, 1)
    packed = pack(subgrid_of_block, live_blocks, coords, block_visibilities, workers)
    arrived = lax.all_to_all(packed, "work", split_axis=0, concat_axis=0, tiled=True)
    labels = arrived[:, FIELDS * SUBW, :SUBW].astype(jnp.int32).reshape(workers * SUBW)
    local_corners = lax.dynamic_slice_in_dim(corners, worker * SUBW, SUBW, 0)
    local_corners = local_corners - jnp.stack([0 * worker, worker * GCW])[None, :]
    planes = []
    for ch in range(CH):
        strip = channel_strip(ch, labels, channel_scale, local_corners, arrived, tiles)
        gathered = lax.all_to_all(strip, "tile", split_axis=0, concat_axis=0, tiled=True)
        planes.append(gathered.sum(axis=0))
    return jnp.concatenate(planes, axis=0)


def solution(mesh):
    return jax.shard_map(
        local,
        mesh=mesh,
        in_specs=(
            P(("work", "tile"), None, None),
            P(("work", "tile"), None, None),
            P(("work", "tile")),
            P(("work", "tile")),
            P(),
            P(),
        ),
        out_specs=P(None, "tile", "work"),
        check_vma=False,
    )
```

```python
import functools
import math

import jax
import jax.numpy as jnp
import numpy as np
from jax import lax
from jax.experimental import pallas as pl
from jax.experimental.pallas import tpu as pltpu
from jax.sharding import PartitionSpec as P

CH = 2
SUB = 32
HALF = SUB // 2
ROWS = 128
TR = 64
GCW = 128
SUBW = 16
FIELDS = 3 + 2 * CH
TERMS = 4 * HALF
GROUP = 8
SPAN = 2
UNROLL = 8

def pack_kernel(label_ref, live_ref, coords_ref, waves_ref, out_ref, count_ref):
    workers, capacity = out_ref.shape[0], SUBW
    out_ref[...] = jnp.zeros_like(out_ref)

    def clear(worker, carry):
        count_ref[worker] = 0
        return carry

    lax.fori_loop(0, workers, clear, 0)
    lane = lax.broadcasted_iota(jnp.int32, (1, ROWS), 1)

    live = live_ref[0]

    def move(group, carry):
        for offset in range(UNROLL):
            block = group * UNROLL + offset
            label = label_ref[block]
            worker = label // SUBW
            slot = count_ref[worker]
            count_ref[worker] = slot + 1
            kept = jnp.where(block < live, 1.0, 0.0)
            for field in range(3):
                out_ref[worker, pl.ds(field * capacity + slot, 1), :] = coords_ref[
                    field, pl.ds(block, 1), :
                ]
            for field in range(2 * CH):
                out_ref[worker, pl.ds((3 + field) * capacity + slot, 1), :] = (
                    waves_ref[block, pl.ds(field, 1), :] * kept
                )
            row = pl.ds(FIELDS * capacity, 1)
            inside = (label - worker * SUBW + 1).astype(jnp.float32) * kept
            out_ref[worker, row, :] = jnp.where(lane == slot, inside, out_ref[worker, row, :])
        return carry

    lax.fori_loop(0, label_ref.shape[0] // UNROLL, move, 0)


def pack(labels, live, coords, waves, workers):
    smem = pl.BlockSpec(memory_space=pltpu.SMEM)
    vmem = pl.BlockSpec(memory_space=pltpu.VMEM)
    return pl.pallas_call(
        pack_kernel,
        name="pack",
        out_shape=jax.ShapeDtypeStruct((workers, FIELDS * SUBW + 8, ROWS), jnp.float32),
        in_specs=[smem, smem, vmem, vmem],
        out_specs=vmem,
        scratch_shapes=[pltpu.SMEM((workers,), jnp.int32)],
    )(labels, live, coords, waves)


def series(square, first, count):
    terms = [(-1.0) ** n / math.factorial(2 * n + first) for n in range(count)]
    total = square * terms[-1] + terms[-2]
    for term in terms[-3::-1]:
        total = total * square + term
    return total


def sin_cos(theta, sin_terms, cos_terms):
    square = theta * theta
    return series(square, 0, cos_terms), series(square, 1, sin_terms) * theta


def times(a, b):
    return a[0] * b[0] - a[1] * b[1], a[0] * b[1] + a[1] * b[0]


def split(value):
    high = value.astype(jnp.bfloat16)
    low = (value - high.astype(jnp.float32)).astype(jnp.bfloat16)
    return high, low


def advance(current, previous, twice_sine):
    return (
        previous[0] - twice_sine * current[1],
        previous[1] + twice_sine * current[0],
    )


def exchange(value):
    return pltpu.roll(value, GROUP // 2, 0)


def interleave(even, odd, low):
    return (
        jnp.where(low, even, exchange(odd)),
        jnp.where(low, exchange(even), odd),
    )


def interleave_pair(even, odd, low):
    real, imag = interleave(even[0], odd[0], low), interleave(even[1], odd[1], low)
    return (real[0], imag[0]), (real[1], imag[1])


def factor_rows(fields, factor, low, put_left, put_right):
    u, v, w = fields[:3]
    first = u * (factor * (2.0 * math.pi / (2 * SUB)))
    second = v * (factor * (2.0 * math.pi / (2 * SUB)))
    depth = w * (factor * (math.pi / (SUB * SUB)))
    along_u = sin_cos(first - depth, 5, 5)
    along_v = sin_cos(second - depth, 5, 5)
    turn = sin_cos(depth * 4.0, 3, 3)
    whole_u, whole_v = times(along_u, along_u), times(along_v, along_v)
    turn2 = times(turn, turn)
    turn3 = times(turn2, turn)
    both = times(along_u, along_v)
    wave = times(fields[3:], (both[0], -both[1]))
    one, zero = jnp.ones_like(u), jnp.zeros_like(u)
    all_u = interleave_pair(along_u, times(whole_u, along_u), low)
    all_v = interleave_pair(along_v, times(whole_v, along_v), low)
    all_wave = interleave_pair(wave, times(wave, turn), low)
    all_chirp = interleave_pair((one, zero), turn, low)
    all_grown = interleave_pair(turn3, times(turn3, turn2), low)
    all_before = interleave_pair((turn[0], -turn[1]), turn, low)
    twice_u = interleave(*[whole_u[0] * whole_u[1] * 4.0] * 2, low)
    twice_v = interleave(*[whole_v[0] * whole_v[1] * 4.0] * 2, low)
    twice_w = interleave(*[turn2[0] * turn2[1] * 4.0] * 2, low)
    for half in range(2):
        along_u, along_v = all_u[half], all_v[half]
        wave, chirp = all_wave[half], all_chirp[half]
        grown, before_grown = all_grown[half], all_before[half]
        before_u = (exchange(along_u[0]), -exchange(along_u[1]))
        before_v = (exchange(along_v[0]), -exchange(along_v[1]))
        for k in range(HALF // 2):
            if k > 0:
                chirp = times(chirp, grown)
                wave = times(wave, grown)
                along_u, before_u = advance(along_u, before_u, twice_u[half]), along_u
                along_v, before_v = advance(along_v, before_v, twice_v[half]), along_v
                grown, before_grown = advance(grown, before_grown, twice_w[half]), grown
            put_left(half, 0, k, wave[0] * along_u[0])
            put_left(half, 1, k, wave[1] * along_u[0])
            put_left(half, 2, k, wave[0] * along_u[1])
            put_left(half, 3, k, wave[1] * along_u[1])
            put_right(half, 0, k, chirp[0] * along_v[0])
            put_right(half, 1, k, chirp[1] * along_v[0])
            put_right(half, 2, k, chirp[0] * along_v[1])
            put_right(half, 3, k, chirp[1] * along_v[1])


def product(left, right, contract):
    left_high, left_low = split(left)
    right_high, right_low = split(right)
    return lax.dot_general(
        jnp.concatenate([left_high, left_high, left_low], axis=1),
        jnp.concatenate([right_high, right_low, right_high], axis=contract),
        (((1,), (contract,)), ((), ())),
        preferred_element_type=jnp.float32,
    )


def picture_kernel(
    ch,
    label_ref,
    scale_ref,
    corner_ref,
    x_ref,
    mix_ref,
    spread_ref,
    out_ref,
    left,
    right,
    sums,
    mixed,
    wide,
    strip,
):
    step = pl.program_id(0)
    capacity = SUBW
    tiles = out_ref.shape[0]
    part = GROUP // 2

    @pl.when(step == 0)
    def _():
        sums[...] = jnp.zeros_like(sums)

    low = lax.broadcasted_iota(jnp.int32, (GROUP, ROWS), 0) < part
    units = [
        (source, group) for source in range(x_ref.shape[0]) for group in range(capacity // GROUP)
    ]

    def factors(unit):
        source, group = units[unit]

        def field(index):
            start = index * capacity + group * GROUP
            return x_ref[source, start : start + GROUP, :]

        def put(ref, half, kind, k, value):
            ref[unit, half, pl.ds(kind * HALF * part + k * GROUP, GROUP), :] = value

        chosen = [field(index) for index in (0, 1, 2, 3 + 2 * ch, 4 + 2 * ch)]
        factor_rows(
            chosen, scale_ref[ch], low, functools.partial(put, left), functools.partial(put, right)
        )

    def gather(unit):
        for slot in range(GROUP):
            label = jnp.maximum(label_ref[(step * len(units) + unit) * GROUP + slot], 0)
            rows = pl.ds(slot % part, TERMS, stride=part)
            half = slot // part
            sums[label] += product(left[unit, half, rows, :], right[unit, half, rows, :], 1)

    def run(chosen):
        factors(chosen[0])
        for before, unit in zip(chosen[:-1], chosen[1:]):
            factors(unit)
            gather(before)
        gather(chosen[-1])

    first_units = [unit for unit in range(len(units)) if units[unit][1] == 0]
    later_units = [unit for unit in range(len(units)) if units[unit][1] > 0]
    crowded = functools.reduce(
        jnp.logical_or,
        [label_ref[(step * len(units) + unit) * GROUP] >= 0 for unit in later_units],
    )

    @pl.when(crowded)
    def _():
        run(list(range(len(units))))

    @pl.when(jnp.logical_not(crowded))
    def _():
        run(first_units)

    @pl.when(step == pl.num_programs(0) - 1)
    def _():
        strip[...] = jnp.zeros_like(strip)
        for subgrid in range(SUBW):
            mixed[subgrid * 2 * SUB : (subgrid + 1) * 2 * SUB, :] = product(
                mix_ref[...], sums[subgrid], 0
            )
        wide[...] = product(mixed[...], spread_ref[...], 0)
        for subgrid in range(SUBW):
            shift = corner_ref[subgrid, 1]
            rows = pl.ds(corner_ref[subgrid, 0], SUB)
            top = pl.ds(subgrid * 2 * SUB, SUB)
            bottom = pl.ds(subgrid * 2 * SUB + SUB, SUB)
            real = wide[top, :GCW] - wide[bottom, GCW:]
            imag = wide[top, GCW:] + wide[bottom, :GCW]
            strip[0, rows, :] += pltpu.roll(real, shift, 1)
            strip[1, rows, :] += pltpu.roll(imag, shift, 1)
        for tile in range(tiles):
            for plane in range(2):
                out_ref[tile, plane] = strip[plane, tile * TR : (tile + 1) * TR, :]


def transform_tables():
    k = np.arange(SUB)[:, None]
    h = np.arange(HALF)[None, :]

    def tapered(x):
        return np.sin(np.pi * (x + 0.5) / SUB) ** 2 * np.exp(-2j * np.pi * k * x / SUB)

    upper, lower = tapered(HALF + h), tapered(HALF - 1 - h)
    even, odd = upper + lower, upper - lower
    table = np.concatenate([even, 1j * even, 1j * odd, -odd], axis=1)
    real, imag = table.real, table.imag
    mix = np.concatenate([real, imag], axis=0) / (ROWS * SUB)
    spread = np.zeros((TERMS, 2 * GCW))
    spread[:, :SUB] = real.T
    spread[:, GCW : GCW + SUB] = imag.T
    return mix.astype(np.float32), spread.astype(np.float32)


def channel_strip(ch, labels, scale, corners, arrived, tiles):
    sources = arrived.shape[0]
    mix, spread = transform_tables()
    parts = (SPAN * SUBW // GROUP, 2, TERMS * GROUP // 2, ROWS)
    return pl.pallas_call(
        functools.partial(picture_kernel, ch),
        name="pictures",
        out_shape=jax.ShapeDtypeStruct((tiles, 2, TR, GCW), jnp.float32),
        grid_spec=pltpu.PrefetchScalarGridSpec(
            num_scalar_prefetch=3,
            grid=(sources // SPAN,),
            in_specs=[
                pl.BlockSpec((SPAN, arrived.shape[1], ROWS), lambda i, *_: (i, 0, 0)),
                pl.BlockSpec(mix.shape, lambda i, *_: (0, 0)),
                pl.BlockSpec(spread.shape, lambda i, *_: (0, 0)),
            ],
            out_specs=pl.BlockSpec((tiles, 2, TR, GCW), lambda i, *_: (0, 0, 0, 0)),
            scratch_shapes=[
                pltpu.VMEM(parts, jnp.float32),
                pltpu.VMEM(parts, jnp.float32),
                pltpu.VMEM((SUBW, TERMS, TERMS), jnp.float32),
                pltpu.VMEM((SUBW * 2 * SUB, TERMS), jnp.float32),
                pltpu.VMEM((SUBW * 2 * SUB, 2 * GCW), jnp.float32),
                pltpu.VMEM((2, TR * tiles, GCW), jnp.float32),
            ],
        ),
        compiler_params=pltpu.CompilerParams(
            dimension_semantics=("arbitrary",), vmem_limit_bytes=20 << 20
        ),
        cost_estimate=pl.CostEstimate(
            flops=3 * 2 * sources * SUBW * TERMS * TERMS * ROWS,
            bytes_accessed=4 * (arrived.size + tiles * 2 * TR * GCW),
            transcendentals=0,
        ),
    )(labels, scale, corners, arrived, jnp.asarray(mix), jnp.asarray(spread))


def local(block_coords, block_visibilities, subgrid_of_block, live_blocks, corners, channel_scale):
    workers = lax.axis_size("work")
    tiles = lax.axis_size("tile")
    worker = lax.axis_index("work")
    coords = jnp.swapaxes(block_coords, 0, 1)
    packed = pack(subgrid_of_block, live_blocks, coords, block_visibilities, workers)
    arrived = lax.all_to_all(packed, "work", split_axis=0, concat_axis=0, tiled=True)
    labels = arrived[:, FIELDS * SUBW, :SUBW].astype(jnp.int32).reshape(workers * SUBW) - 1
    local_corners = lax.dynamic_slice_in_dim(corners, worker * SUBW, SUBW, 0)
    local_corners = local_corners - jnp.stack([0 * worker, worker * GCW])[None, :]
    planes = []
    for ch in range(CH):
        strip = channel_strip(ch, labels, channel_scale, local_corners, arrived, tiles)
        gathered = lax.all_to_all(strip, "tile", split_axis=0, concat_axis=0, tiled=True)
        planes.append(gathered.sum(axis=0))
    return jnp.concatenate(planes, axis=0)


def solution(mesh):
    return jax.shard_map(
        local,
        mesh=mesh,
        in_specs=(
            P(("work", "tile"), None, None),
            P(("work", "tile"), None, None),
            P(("work", "tile")),
            P(("work", "tile")),
            P(),
            P(),
        ),
        out_specs=P(None, "tile", "work"),
        check_vma=False,
    )
```

```python
import functools
import math

import jax
import jax.numpy as jnp
import numpy as np
from jax import lax
from jax.experimental import pallas as pl
from jax.experimental.pallas import tpu as pltpu
from jax.sharding import PartitionSpec as P


CH = 2
SUB = 32
HALF = SUB // 2
ROWS = 128
TR = 64
GCW = 128
SUBW = 16
FIELDS = 3 + 2 * CH
TERMS = 4 * HALF
GROUP = 8
SPAN = 4
CHUNKS = SUBW // GROUP
UNROLL = 8


def pack_kernel(label_ref, live_ref, coords_ref, waves_ref, *refs):
    out_refs, (room, count_ref) = refs[:CHUNKS], refs[CHUNKS:]
    workers = room.shape[1]
    room[...] = jnp.zeros_like(room)

    def clear(worker, carry):
        count_ref[worker] = 0
        return carry

    lax.fori_loop(0, workers, clear, 0)
    lane = lax.broadcasted_iota(jnp.int32, (1, ROWS), 1)
    live = live_ref[0]

    def move(group, carry):
        for offset in range(UNROLL):
            block = group * UNROLL + offset
            label = label_ref[block]
            worker = label // SUBW
            count = count_ref[worker]
            count_ref[worker] = count + 1
            chunk, slot = count // GROUP, count % GROUP
            kept = jnp.where(block < live, 1.0, 0.0)
            for field in range(3):
                room[chunk, worker, pl.ds(field * GROUP + slot, 1), :] = coords_ref[
                    field, pl.ds(block, 1), :
                ]
            for field in range(2 * CH):
                room[chunk, worker, pl.ds((3 + field) * GROUP + slot, 1), :] = (
                    waves_ref[block, pl.ds(field, 1), :] * kept
                )
            row = pl.ds(FIELDS * GROUP, 1)
            inside = (label - worker * SUBW + 1).astype(jnp.float32) * kept
            room[chunk, worker, row, :] = jnp.where(
                lane == slot, inside, room[chunk, worker, row, :]
            )
        return carry

    lax.fori_loop(0, label_ref.shape[0] // UNROLL, move, 0)
    for chunk in range(CHUNKS):
        out_refs[chunk][...] = room[chunk]


def pack(labels, live, coords, waves, workers):
    smem = pl.BlockSpec(memory_space=pltpu.SMEM)
    vmem = pl.BlockSpec(memory_space=pltpu.VMEM)
    shape = (workers, (FIELDS + 1) * GROUP, ROWS)
    return pl.pallas_call(
        pack_kernel,
        name="pack",
        out_shape=[jax.ShapeDtypeStruct(shape, jnp.float32)] * CHUNKS,
        in_specs=[smem, smem, vmem, vmem],
        out_specs=[vmem] * CHUNKS,
        scratch_shapes=[
            pltpu.VMEM((CHUNKS,) + shape, jnp.float32),
            pltpu.SMEM((workers,), jnp.int32),
        ],
    )(labels, live, coords, waves)


def series(square, first, count):
    terms = [(-1.0) ** n / math.factorial(2 * n + first) for n in range(count)]
    total = square * terms[-1] + terms[-2]
    for term in terms[-3::-1]:
        total = total * square + term
    return total


def sin_cos(theta, sin_terms, cos_terms):
    square = theta * theta
    return series(square, 0, cos_terms), series(square, 1, sin_terms) * theta


def times(a, b):
    return a[0] * b[0] - a[1] * b[1], a[0] * b[1] + a[1] * b[0]


def split(value):
    high = value.astype(jnp.bfloat16)
    low = (value - high.astype(jnp.float32)).astype(jnp.bfloat16)
    return high, low


def advance(current, previous, twice_sine):
    return (
        previous[0] - twice_sine * current[1],
        previous[1] + twice_sine * current[0],
    )


def exchange(value):
    return pltpu.roll(value, GROUP // 2, 0)


def interleave(even, odd, low):
    return (
        jnp.where(low, even, exchange(odd)),
        jnp.where(low, exchange(even), odd),
    )


def interleave_pair(even, odd, low):
    real, imag = interleave(even[0], odd[0], low), interleave(even[1], odd[1], low)
    return (real[0], imag[0]), (real[1], imag[1])


def factor_rows(fields, factor, low, put_left, put_right):
    u, v, w = fields[:3]
    first = u * (factor * (2.0 * math.pi / (2 * SUB)))
    second = v * (factor * (2.0 * math.pi / (2 * SUB)))
    depth = w * (factor * (math.pi / (SUB * SUB)))
    along_u = sin_cos(first - depth, 5, 5)
    along_v = sin_cos(second - depth, 5, 5)
    turn = sin_cos(depth * 4.0, 3, 3)
    whole_u, whole_v = times(along_u, along_u), times(along_v, along_v)
    turn2 = times(turn, turn)
    turn3 = times(turn2, turn)
    both = times(along_u, along_v)
    wave = times(fields[3:], (both[0], -both[1]))
    one, zero = jnp.ones_like(u), jnp.zeros_like(u)
    all_u = interleave_pair(along_u, times(whole_u, along_u), low)
    all_v = interleave_pair(along_v, times(whole_v, along_v), low)
    all_wave = interleave_pair(wave, times(wave, turn), low)
    all_chirp = interleave_pair((one, zero), turn, low)
    all_grown = interleave_pair(turn3, times(turn3, turn2), low)
    all_before = interleave_pair((turn[0], -turn[1]), turn, low)
    twice_u = interleave(*[whole_u[0] * whole_u[1] * 4.0] * 2, low)
    twice_v = interleave(*[whole_v[0] * whole_v[1] * 4.0] * 2, low)
    twice_w = interleave(*[turn2[0] * turn2[1] * 4.0] * 2, low)
    for half in range(2):
        along_u, along_v = all_u[half], all_v[half]
        wave, chirp = all_wave[half], all_chirp[half]
        grown, before_grown = all_grown[half], all_before[half]
        before_u = (exchange(along_u[0]), -exchange(along_u[1]))
        before_v = (exchange(along_v[0]), -exchange(along_v[1]))
        for k in range(HALF // 2):
            if k > 0:
                chirp = times(chirp, grown)
                wave = times(wave, grown)
                along_u, before_u = advance(along_u, before_u, twice_u[half]), along_u
                along_v, before_v = advance(along_v, before_v, twice_v[half]), along_v
                grown, before_grown = advance(grown, before_grown, twice_w[half]), grown
            put_left(half, 0, k, wave[0] * along_u[0])
            put_left(half, 1, k, wave[1] * along_u[0])
            put_left(half, 2, k, wave[0] * along_u[1])
            put_left(half, 3, k, wave[1] * along_u[1])
            put_right(half, 0, k, chirp[0] * along_v[0])
            put_right(half, 1, k, chirp[1] * along_v[0])
            put_right(half, 2, k, chirp[0] * along_v[1])
            put_right(half, 3, k, chirp[1] * along_v[1])


def product(left, right, contract):
    left_high, left_low = split(left)
    right_high, right_low = split(right)
    return lax.dot_general(
        jnp.concatenate([left_high, left_high, left_low], axis=1),
        jnp.concatenate([right_high, right_low, right_high], axis=contract),
        (((1,), (contract,)), ((), ())),
        preferred_element_type=jnp.float32,
    )


def accumulate(label_ref, scale_ref, x_ref, left, right, sums):
    step = pl.program_id(0)
    part = GROUP // 2
    sources = x_ref.shape[0]
    low = lax.broadcasted_iota(jnp.int32, (GROUP, ROWS), 0) < part

    def factors(source, ch):
        def field(index):
            return x_ref[source, index * GROUP : (index + 1) * GROUP, :]

        def put(ref, half, kind, k, value):
            ref[source, ch, half, pl.ds(kind * HALF * part + k * GROUP, GROUP), :] = value

        chosen = [field(index) for index in (0, 1, 2, 3 + 2 * ch, 4 + 2 * ch)]
        factor_rows(
            chosen, scale_ref[ch], low, functools.partial(put, left), functools.partial(put, right)
        )

    def gather(source, ch):
        for slot in range(GROUP):
            label = jnp.maximum(label_ref[(step * sources + source) * GROUP + slot], 0)
            rows = pl.ds(slot % part, TERMS, stride=part)
            half = slot // part
            sums[ch, label] += product(
                left[source, ch, half, rows, :], right[source, ch, half, rows, :], 1
            )

    live = functools.reduce(
        jnp.logical_or,
        [label_ref[(step * sources + source) * GROUP] >= 0 for source in range(sources)],
    )

    @pl.when(live)
    def _():
        units = [(source, ch) for source in range(sources) for ch in range(CH)]
        factors(*units[0])
        for before, unit in zip(units[:-1], units[1:]):
            factors(*unit)
            gather(*before)
        gather(*units[-1])


def first_kernel(label_ref, scale_ref, x_ref, sums, left, right):
    @pl.when(pl.program_id(0) == 0)
    def _():
        sums[...] = jnp.zeros_like(sums)

    accumulate(label_ref, scale_ref, x_ref, left, right, sums)


def last_kernel(
    label_ref,
    scale_ref,
    corner_ref,
    x_ref,
    prior_ref,
    mix_ref,
    spread_ref,
    out_ref,
    left,
    right,
    sums,
    mixed,
    wide,
    strip,
):
    tiles = out_ref.shape[0]

    @pl.when(pl.program_id(0) == 0)
    def _():
        sums[...] = prior_ref[...]

    accumulate(label_ref, scale_ref, x_ref, left, right, sums)

    @pl.when(pl.program_id(0) == pl.num_programs(0) - 1)
    def _():
        strip[...] = jnp.zeros_like(strip)
        for ch in range(CH):
            for subgrid in range(SUBW):
                mixed[ch, subgrid * 2 * SUB : (subgrid + 1) * 2 * SUB, :] = product(
                    mix_ref[...], sums[ch, subgrid], 0
                )
            wide[ch] = product(mixed[ch], spread_ref[...], 0)
            for subgrid in range(SUBW):
                shift = corner_ref[subgrid, 1]
                rows = pl.ds(corner_ref[subgrid, 0], SUB)
                top = pl.ds(subgrid * 2 * SUB, SUB)
                bottom = pl.ds(subgrid * 2 * SUB + SUB, SUB)
                real = wide[ch, top, :GCW] - wide[ch, bottom, GCW:]
                imag = wide[ch, top, GCW:] + wide[ch, bottom, :GCW]
                strip[2 * ch, rows, :] += pltpu.roll(real, shift, 1)
                strip[2 * ch + 1, rows, :] += pltpu.roll(imag, shift, 1)
        for tile in range(tiles):
            for plane in range(2 * CH):
                out_ref[tile, plane] = strip[plane, tile * TR : (tile + 1) * TR, :]


def transform_tables():
    k = np.arange(SUB)[:, None]
    h = np.arange(HALF)[None, :]

    def tapered(x):
        return np.sin(np.pi * (x + 0.5) / SUB) ** 2 * np.exp(-2j * np.pi * k * x / SUB)

    upper, lower = tapered(HALF + h), tapered(HALF - 1 - h)
    even, odd = upper + lower, upper - lower
    table = np.concatenate([even, 1j * even, 1j * odd, -odd], axis=1)
    real, imag = table.real, table.imag
    mix = np.concatenate([real, imag], axis=0) / (ROWS * SUB)
    spread = np.zeros((TERMS, 2 * GCW))
    spread[:, :SUB] = real.T
    spread[:, GCW : GCW + SUB] = imag.T
    return mix.astype(np.float32), spread.astype(np.float32)


SUMS = (CH, SUBW, TERMS, TERMS)
ROOM = (SPAN, CH, 2, TERMS * GROUP // 2, ROWS)


def chunk_call(kernel, prefetched, arrived, extra, out_shape, scratch):
    sources = arrived.shape[0]
    whole = [pl.BlockSpec(x.shape, lambda i, *_, n=x.ndim: (0,) * n) for x in extra]
    return pl.pallas_call(
        kernel,
        out_shape=jax.ShapeDtypeStruct(out_shape, jnp.float32),
        grid_spec=pltpu.PrefetchScalarGridSpec(
            num_scalar_prefetch=len(prefetched),
            grid=(sources // SPAN,),
            in_specs=[pl.BlockSpec((SPAN, arrived.shape[1], ROWS), lambda i, *_: (i, 0, 0))]
            + whole,
            out_specs=pl.BlockSpec(out_shape, lambda i, *_: (0,) * len(out_shape)),
            scratch_shapes=[pltpu.VMEM(shape, jnp.float32) for shape in [ROOM, ROOM] + scratch],
        ),
        compiler_params=pltpu.CompilerParams(
            dimension_semantics=("arbitrary",), vmem_limit_bytes=28 << 20
        ),
        cost_estimate=pl.CostEstimate(
            flops=3 * 2 * CH * sources * GROUP * TERMS * TERMS * ROWS,
            bytes_accessed=4 * (arrived.size + math.prod(out_shape)),
            transcendentals=0,
        ),
    )(*prefetched, arrived, *extra)


def local(block_coords, block_visibilities, subgrid_of_block, live_blocks, corners, channel_scale):
    workers = lax.axis_size("work")
    tiles = lax.axis_size("tile")
    worker = lax.axis_index("work")
    coords = jnp.swapaxes(block_coords, 0, 1)
    packed = pack(subgrid_of_block, live_blocks, coords, block_visibilities, workers)
    local_corners = lax.dynamic_slice_in_dim(corners, worker * SUBW, SUBW, 0)
    local_corners = local_corners - jnp.stack([0 * worker, worker * GCW])[None, :]
    sums = None
    for chunk in range(CHUNKS):
        arrived = lax.all_to_all(packed[chunk], "work", split_axis=0, concat_axis=0, tiled=True)
        labels = arrived[:, FIELDS * GROUP, :GROUP].astype(jnp.int32).reshape(workers * GROUP) - 1
        if chunk == 0:
            sums = chunk_call(first_kernel, (labels, channel_scale), arrived, (), SUMS, [])
    mix, spread = transform_tables()
    strip = chunk_call(
        last_kernel,
        (labels, channel_scale, local_corners),
        arrived,
        (sums, jnp.asarray(mix), jnp.asarray(spread)),
        (tiles, 2 * CH, TR, GCW),
        [
            SUMS,
            (CH, SUBW * 2 * SUB, TERMS),
            (CH, SUBW * 2 * SUB, 2 * GCW),
            (2 * CH, TR * tiles, GCW),
        ],
    )
    gathered = lax.all_to_all(strip, "tile", split_axis=0, concat_axis=0, tiled=True)
    return gathered.sum(axis=0)


def solution(mesh):
    return jax.shard_map(
        local,
        mesh=mesh,
        in_specs=(
            P(("work", "tile"), None, None),
            P(("work", "tile"), None, None),
            P(("work", "tile")),
            P(("work", "tile")),
            P(),
            P(),
        ),
        out_specs=P(None, "tile", "work"),
        check_vma=False,
    )
```

```python
import functools
import math

import jax
import jax.numpy as jnp
import numpy as np
from jax import lax
from jax.experimental import pallas as pl
from jax.experimental.pallas import tpu as pltpu
from jax.sharding import PartitionSpec as P


CH = 2
SUB = 32
HALF = SUB // 2
ROWS = 128
TR = 64
GCW = 128
SUBW = 16
FIELDS = 3 + 2 * CH
TERMS = 4 * HALF
GROUP = 8
SPAN = 4
CHUNKS = SUBW // GROUP
UNROLL = 8


def pack_kernel(label_ref, live_ref, coords_ref, waves_ref, *refs):
    out_refs, (room, count_ref) = refs[:CHUNKS], refs[CHUNKS:]
    workers = room.shape[1]
    room[...] = jnp.zeros_like(room)

    def clear(worker, carry):
        count_ref[worker] = 0
        return carry

    lax.fori_loop(0, workers, clear, 0)
    lane = lax.broadcasted_iota(jnp.int32, (1, ROWS), 1)
    live = live_ref[0]

    def move(group, carry):
        for offset in range(UNROLL):
            block = group * UNROLL + offset
            label = label_ref[block]
            worker = label // SUBW
            count = count_ref[worker]
            count_ref[worker] = count + 1
            chunk, slot = count // GROUP, count % GROUP
            kept = jnp.where(block < live, 1.0, 0.0)
            for field in range(3):
                room[chunk, worker, pl.ds(field * GROUP + slot, 1), :] = coords_ref[
                    field, pl.ds(block, 1), :
                ]
            for field in range(2 * CH):
                room[chunk, worker, pl.ds((3 + field) * GROUP + slot, 1), :] = (
                    waves_ref[block, pl.ds(field, 1), :] * kept
                )
            row = pl.ds(FIELDS * GROUP, 1)
            inside = (label - worker * SUBW + 1).astype(jnp.float32) * kept
            room[chunk, worker, row, :] = jnp.where(
                lane == slot, inside, room[chunk, worker, row, :]
            )
        return carry

    lax.fori_loop(0, label_ref.shape[0] // UNROLL, move, 0)
    for chunk in range(CHUNKS):
        out_refs[chunk][...] = room[chunk]


def pack(labels, live, coords, waves, workers):
    smem = pl.BlockSpec(memory_space=pltpu.SMEM)
    vmem = pl.BlockSpec(memory_space=pltpu.VMEM)
    shape = (workers, (FIELDS + 1) * GROUP, ROWS)
    return pl.pallas_call(
        pack_kernel,
        name="pack",
        out_shape=[jax.ShapeDtypeStruct(shape, jnp.float32)] * CHUNKS,
        in_specs=[smem, smem, vmem, vmem],
        out_specs=[vmem] * CHUNKS,
        scratch_shapes=[
            pltpu.VMEM((CHUNKS,) + shape, jnp.float32),
            pltpu.SMEM((workers,), jnp.int32),
        ],
    )(labels, live, coords, waves)


def series(square, first, count):
    terms = [(-1.0) ** n / math.factorial(2 * n + first) for n in range(count)]
    total = square * terms[-1] + terms[-2]
    for term in terms[-3::-1]:
        total = total * square + term
    return total


def sin_cos(theta, sin_terms, cos_terms):
    square = theta * theta
    return series(square, 0, cos_terms), series(square, 1, sin_terms) * theta


def times(a, b):
    return a[0] * b[0] - a[1] * b[1], a[0] * b[1] + a[1] * b[0]


def split(value):
    high = value.astype(jnp.bfloat16)
    low = (value - high.astype(jnp.float32)).astype(jnp.bfloat16)
    return high, low


def advance(current, previous, twice_sine):
    return (
        previous[0] - twice_sine * current[1],
        previous[1] + twice_sine * current[0],
    )


def exchange(value):
    return pltpu.roll(value, GROUP // 2, 0)


def interleave(even, odd, low):
    return (
        jnp.where(low, even, exchange(odd)),
        jnp.where(low, exchange(even), odd),
    )


def interleave_pair(even, odd, low):
    real, imag = interleave(even[0], odd[0], low), interleave(even[1], odd[1], low)
    return (real[0], imag[0]), (real[1], imag[1])


def factor_rows(fields, factor, low, put_left, put_right):
    u, v, w = fields[:3]
    first = u * (factor * (2.0 * math.pi / (2 * SUB)))
    second = v * (factor * (2.0 * math.pi / (2 * SUB)))
    depth = w * (factor * (math.pi / (SUB * SUB)))
    along_u = sin_cos(first - depth, 5, 5)
    along_v = sin_cos(second - depth, 5, 5)
    turn = sin_cos(depth * 4.0, 3, 3)
    whole_u, whole_v = times(along_u, along_u), times(along_v, along_v)
    turn2 = times(turn, turn)
    turn3 = times(turn2, turn)
    both = times(along_u, along_v)
    wave = times(fields[3:], (both[0], -both[1]))
    one, zero = jnp.ones_like(u), jnp.zeros_like(u)
    all_u = interleave_pair(along_u, times(whole_u, along_u), low)
    all_v = interleave_pair(along_v, times(whole_v, along_v), low)
    all_wave = interleave_pair(wave, times(wave, turn), low)
    all_chirp = interleave_pair((one, zero), turn, low)
    all_grown = interleave_pair(turn3, times(turn3, turn2), low)
    all_before = interleave_pair((turn[0], -turn[1]), turn, low)
    twice_u = interleave(*[whole_u[0] * whole_u[1] * 4.0] * 2, low)
    twice_v = interleave(*[whole_v[0] * whole_v[1] * 4.0] * 2, low)
    twice_w = interleave(*[turn2[0] * turn2[1] * 4.0] * 2, low)
    for half in range(2):
        along_u, along_v = all_u[half], all_v[half]
        wave, chirp = all_wave[half], all_chirp[half]
        grown, before_grown = all_grown[half], all_before[half]
        before_u = (exchange(along_u[0]), -exchange(along_u[1]))
        before_v = (exchange(along_v[0]), -exchange(along_v[1]))
        for k in range(HALF // 2):
            if k > 0:
                chirp = times(chirp, grown)
                wave = times(wave, grown)
                along_u, before_u = advance(along_u, before_u, twice_u[half]), along_u
                along_v, before_v = advance(along_v, before_v, twice_v[half]), along_v
                grown, before_grown = advance(grown, before_grown, twice_w[half]), grown
            put_left(half, 0, k, wave[0] * along_u[0])
            put_left(half, 1, k, wave[1] * along_u[0])
            put_left(half, 2, k, wave[0] * along_u[1])
            put_left(half, 3, k, wave[1] * along_u[1])
            put_right(half, 0, k, chirp[0] * along_v[0])
            put_right(half, 1, k, chirp[1] * along_v[0])
            put_right(half, 2, k, chirp[0] * along_v[1])
            put_right(half, 3, k, chirp[1] * along_v[1])


def product(left, right, contract):
    left_high, left_low = split(left)
    right_high, right_low = split(right)
    return lax.dot_general(
        jnp.concatenate([left_high, left_high, left_low], axis=1),
        jnp.concatenate([right_high, right_low, right_high], axis=contract),
        (((1,), (contract,)), ((), ())),
        preferred_element_type=jnp.float32,
    )


def accumulate(label_ref, scale_ref, x_ref, left, right, sums):
    step = pl.program_id(0)
    part = GROUP // 2
    sources = x_ref.shape[0]
    low = lax.broadcasted_iota(jnp.int32, (GROUP, ROWS), 0) < part

    def factors(source, ch):
        def field(index):
            return x_ref[source, index * GROUP : (index + 1) * GROUP, :]

        def put(ref, half, kind, k, value):
            ref[source, ch, half, pl.ds(kind * HALF * part + k * GROUP, GROUP), :] = value

        chosen = [field(index) for index in (0, 1, 2, 3 + 2 * ch, 4 + 2 * ch)]
        factor_rows(
            chosen, scale_ref[ch], low, functools.partial(put, left), functools.partial(put, right)
        )

    def gather(source, ch):
        for slot in range(GROUP):
            label = jnp.maximum(label_ref[(step * sources + source) * GROUP + slot], 0)
            rows = pl.ds(slot % part, TERMS, stride=part)
            half = slot // part
            sums[ch, label] += product(
                left[source, ch, half, rows, :], right[source, ch, half, rows, :], 1
            )

    live = functools.reduce(
        jnp.logical_or,
        [label_ref[(step * sources + source) * GROUP] >= 0 for source in range(sources)],
    )

    @pl.when(live)
    def _():
        units = [(source, ch) for source in range(sources) for ch in range(CH)]
        factors(*units[0])
        for before, unit in zip(units[:-1], units[1:]):
            factors(*unit)
            gather(*before)
        gather(*units[-1])


def first_kernel(label_ref, scale_ref, x_ref, sums, left, right):
    @pl.when(pl.program_id(0) == 0)
    def _():
        sums[...] = jnp.zeros_like(sums)

    accumulate(label_ref, scale_ref, x_ref, left, right, sums)


def last_kernel(
    label_ref,
    scale_ref,
    corner_ref,
    tile_ref,
    x_ref,
    prior_ref,
    mix_ref,
    spread_ref,
    out_ref,
    left,
    right,
    sums,
    mixed,
    wide,
    strip,
):
    tiles = out_ref.shape[0]

    @pl.when(pl.program_id(0) == 0)
    def _():
        sums[...] = prior_ref[...]

    accumulate(label_ref, scale_ref, x_ref, left, right, sums)

    @pl.when(pl.program_id(0) == pl.num_programs(0) - 1)
    def _():
        strip[...] = jnp.zeros_like(strip)
        for ch in range(CH):
            for subgrid in range(SUBW):
                mixed[ch, subgrid * 2 * SUB : (subgrid + 1) * 2 * SUB, :] = product(
                    mix_ref[...], sums[ch, subgrid], 0
                )
            wide[ch] = product(mixed[ch], spread_ref[...], 0)
            for subgrid in range(SUBW):
                shift = corner_ref[subgrid, 1]
                rows = pl.ds(corner_ref[subgrid, 0], SUB)
                top = pl.ds(subgrid * 2 * SUB, SUB)
                bottom = pl.ds(subgrid * 2 * SUB + SUB, SUB)
                real = wide[ch, top, :GCW] - wide[ch, bottom, GCW:]
                imag = wide[ch, top, GCW:] + wide[ch, bottom, :GCW]
                strip[2 * ch, rows, :] += pltpu.roll(real, shift, 1)
                strip[2 * ch + 1, rows, :] += pltpu.roll(imag, shift, 1)
        for distance in range(tiles):
            tile = lax.rem(tile_ref[0] + distance, tiles)
            rows = pl.ds(pl.multiple_of(tile * TR, TR), TR)
            for plane in range(2 * CH):
                out_ref[distance, plane] = strip[plane, rows, :]


def transform_tables():
    k = np.arange(SUB)[:, None]
    h = np.arange(HALF)[None, :]

    def tapered(x):
        return np.sin(np.pi * (x + 0.5) / SUB) ** 2 * np.exp(-2j * np.pi * k * x / SUB)

    upper, lower = tapered(HALF + h), tapered(HALF - 1 - h)
    even, odd = upper + lower, upper - lower
    table = np.concatenate([even, 1j * even, 1j * odd, -odd], axis=1)
    real, imag = table.real, table.imag
    mix = np.concatenate([real, imag], axis=0) / (ROWS * SUB)
    spread = np.zeros((TERMS, 2 * GCW))
    spread[:, :SUB] = real.T
    spread[:, GCW : GCW + SUB] = imag.T
    return mix.astype(np.float32), spread.astype(np.float32)


SUMS = (CH, SUBW, TERMS, TERMS)
ROOM = (SPAN, CH, 2, TERMS * GROUP // 2, ROWS)


def chunk_call(kernel, prefetched, arrived, extra, out_shape, scratch):
    sources = arrived.shape[0]
    whole = [pl.BlockSpec(x.shape, lambda i, *_, n=x.ndim: (0,) * n) for x in extra]
    return pl.pallas_call(
        kernel,
        out_shape=jax.ShapeDtypeStruct(out_shape, jnp.float32),
        grid_spec=pltpu.PrefetchScalarGridSpec(
            num_scalar_prefetch=len(prefetched),
            grid=(sources // SPAN,),
            in_specs=[pl.BlockSpec((SPAN, arrived.shape[1], ROWS), lambda i, *_: (i, 0, 0))]
            + whole,
            out_specs=pl.BlockSpec(out_shape, lambda i, *_: (0,) * len(out_shape)),
            scratch_shapes=[pltpu.VMEM(shape, jnp.float32) for shape in [ROOM, ROOM] + scratch],
        ),
        compiler_params=pltpu.CompilerParams(
            dimension_semantics=("arbitrary",), vmem_limit_bytes=28 << 20
        ),
        cost_estimate=pl.CostEstimate(
            flops=3 * 2 * CH * sources * GROUP * TERMS * TERMS * ROWS,
            bytes_accessed=4 * (arrived.size + math.prod(out_shape)),
            transcendentals=0,
        ),
    )(*prefetched, arrived, *extra)


def summed_around(parts, axis):
    size = lax.axis_size(axis)
    far = size // 2
    up = [(i, (i + 1) % size) for i in range(size)]
    down = [(i, (i - 1) % size) for i in range(size)]
    rising = lax.ppermute(parts[far, :CH], axis, up)
    falling = lax.ppermute(parts[far, CH:], axis, down)
    for distance in range(far - 1, 0, -1):
        near, opposite = parts[distance], parts[size - distance]
        if distance == far - 1:
            rising = jnp.concatenate([near[:CH] + rising, near[CH:]])
            falling = jnp.concatenate([opposite[:CH], opposite[CH:] + falling])
        else:
            rising, falling = near + rising, opposite + falling
        rising = lax.ppermute(rising, axis, up)
        falling = lax.ppermute(falling, axis, down)
    return parts[0] + rising + falling


def local(block_coords, block_visibilities, subgrid_of_block, live_blocks, corners, channel_scale):
    workers = lax.axis_size("work")
    tiles = lax.axis_size("tile")
    worker = lax.axis_index("work")
    coords = jnp.swapaxes(block_coords, 0, 1)
    packed = pack(subgrid_of_block, live_blocks, coords, block_visibilities, workers)
    local_corners = lax.dynamic_slice_in_dim(corners, worker * SUBW, SUBW, 0)
    local_corners = local_corners - jnp.stack([0 * worker, worker * GCW])[None, :]
    sums = None
    for chunk in range(CHUNKS):
        arrived = lax.all_to_all(packed[chunk], "work", split_axis=0, concat_axis=0, tiled=True)
        labels = arrived[:, FIELDS * GROUP, :GROUP].astype(jnp.int32).reshape(workers * GROUP) - 1
        if chunk == 0:
            sums = chunk_call(first_kernel, (labels, channel_scale), arrived, (), SUMS, [])
    mix, spread = transform_tables()
    tile = lax.axis_index("tile").astype(jnp.int32).reshape(1)
    parts = chunk_call(
        last_kernel,
        (labels, channel_scale, local_corners, tile),
        arrived,
        (sums, jnp.asarray(mix), jnp.asarray(spread)),
        (tiles, 2 * CH, TR, GCW),
        [
            SUMS,
            (CH, SUBW * 2 * SUB, TERMS),
            (CH, SUBW * 2 * SUB, 2 * GCW),
            (2 * CH, TR * tiles, GCW),
        ],
    )
    return summed_around(parts, "tile")


def solution(mesh):
    return jax.shard_map(
        local,
        mesh=mesh,
        in_specs=(
            P(("work", "tile"), None, None),
            P(("work", "tile"), None, None),
            P(("work", "tile")),
            P(("work", "tile")),
            P(),
            P(),
        ),
        out_specs=P(None, "tile", "work"),
        check_vma=False,
    )
```

```python
import functools
import math

import jax
import jax.numpy as jnp
import numpy as np
from jax import lax
from jax.experimental import pallas as pl
from jax.experimental.pallas import tpu as pltpu
from jax.sharding import PartitionSpec as P


CH = 2
SUB = 32
HALF = SUB // 2
ROWS = 128
TR = 64
GCW = 128
SUBW = 16
FIELDS = 3 + 2 * CH
TERMS = 4 * HALF
GROUP = 8
SPAN = 8
CHUNKS = SUBW // GROUP
UNROLL = 8


def pack_kernel(chunk, label_ref, live_ref, coords_ref, waves_ref, out_ref, count_ref):
    workers = out_ref.shape[0]
    out_ref[...] = jnp.zeros_like(out_ref)

    def clear(worker, carry):
        count_ref[worker] = 0
        return carry

    lax.fori_loop(0, workers, clear, 0)
    lane = lax.broadcasted_iota(jnp.int32, (1, ROWS), 1)
    live = live_ref[0]

    def move(group, carry):
        for offset in range(UNROLL):
            block = group * UNROLL + offset
            label = label_ref[block]
            worker = label // SUBW
            slot = count_ref[worker] - chunk * GROUP
            count_ref[worker] = slot + chunk * GROUP + 1

            @pl.when((slot >= 0) & (slot < GROUP) & (block < live))
            def _():
                for field in range(3):
                    out_ref[worker, pl.ds(field * GROUP + slot, 1), :] = coords_ref[
                        field, pl.ds(block, 1), :
                    ]
                for field in range(2 * CH):
                    out_ref[worker, pl.ds((3 + field) * GROUP + slot, 1), :] = waves_ref[
                        block, pl.ds(field, 1), :
                    ]
                row = pl.ds(FIELDS * GROUP, 1)
                inside = (label - worker * SUBW + 1).astype(jnp.float32)
                out_ref[worker, row, :] = jnp.where(lane == slot, inside, out_ref[worker, row, :])

        return carry

    lax.fori_loop(0, label_ref.shape[0] // UNROLL, move, 0)


def pack(chunk, labels, live, coords, waves, workers):
    smem = pl.BlockSpec(memory_space=pltpu.SMEM)
    vmem = pl.BlockSpec(memory_space=pltpu.VMEM)
    shape = (workers, (FIELDS + 1) * GROUP, ROWS)
    return pl.pallas_call(
        functools.partial(pack_kernel, chunk),
        name="pack",
        out_shape=jax.ShapeDtypeStruct(shape, jnp.float32),
        in_specs=[smem, smem, vmem, vmem],
        out_specs=vmem,
        scratch_shapes=[pltpu.SMEM((workers,), jnp.int32)],
        cost_estimate=pl.CostEstimate(
            flops=0, bytes_accessed=4 * math.prod(shape), transcendentals=0
        ),
    )(labels, live, coords, waves)


def series(square, first, count):
    terms = [(-1.0) ** n / math.factorial(2 * n + first) for n in range(count)]
    total = square * terms[-1] + terms[-2]
    for term in terms[-3::-1]:
        total = total * square + term
    return total


def sin_cos(theta, sin_terms, cos_terms):
    square = theta * theta
    return series(square, 0, cos_terms), series(square, 1, sin_terms) * theta


def times(a, b):
    return a[0] * b[0] - a[1] * b[1], a[0] * b[1] + a[1] * b[0]


def split(value):
    high = value.astype(jnp.bfloat16)
    low = (value - high.astype(jnp.float32)).astype(jnp.bfloat16)
    return high, low


def advance(current, previous, twice_sine):
    return (
        previous[0] - twice_sine * current[1],
        previous[1] + twice_sine * current[0],
    )


def exchange(value):
    return pltpu.roll(value, GROUP // 2, 0)


def interleave(even, odd, low):
    return (
        jnp.where(low, even, exchange(odd)),
        jnp.where(low, exchange(even), odd),
    )


def interleave_pair(even, odd, low):
    real, imag = interleave(even[0], odd[0], low), interleave(even[1], odd[1], low)
    return (real[0], imag[0]), (real[1], imag[1])


def factor_rows(fields, factor, low, put_left, put_right):
    u, v, w = fields[:3]
    first = u * (factor * (2.0 * math.pi / (2 * SUB)))
    second = v * (factor * (2.0 * math.pi / (2 * SUB)))
    depth = w * (factor * (math.pi / (SUB * SUB)))
    along_u = sin_cos(first - depth, 5, 5)
    along_v = sin_cos(second - depth, 5, 5)
    turn = sin_cos(depth * 4.0, 3, 3)
    whole_u, whole_v = times(along_u, along_u), times(along_v, along_v)
    turn2 = times(turn, turn)
    turn3 = times(turn2, turn)
    both = times(along_u, along_v)
    wave = times(fields[3:], (both[0], -both[1]))
    one, zero = jnp.ones_like(u), jnp.zeros_like(u)
    all_u = interleave_pair(along_u, times(whole_u, along_u), low)
    all_v = interleave_pair(along_v, times(whole_v, along_v), low)
    all_wave = interleave_pair(wave, times(wave, turn), low)
    all_chirp = interleave_pair((one, zero), turn, low)
    all_grown = interleave_pair(turn3, times(turn3, turn2), low)
    all_before = interleave_pair((turn[0], -turn[1]), turn, low)
    twice_u = interleave(*[whole_u[0] * whole_u[1] * 4.0] * 2, low)
    twice_v = interleave(*[whole_v[0] * whole_v[1] * 4.0] * 2, low)
    twice_w = interleave(*[turn2[0] * turn2[1] * 4.0] * 2, low)
    for half in range(2):
        along_u, along_v = all_u[half], all_v[half]
        wave, chirp = all_wave[half], all_chirp[half]
        grown, before_grown = all_grown[half], all_before[half]
        before_u = (exchange(along_u[0]), -exchange(along_u[1]))
        before_v = (exchange(along_v[0]), -exchange(along_v[1]))
        for k in range(HALF // 2):
            if k > 0:
                chirp = times(chirp, grown)
                wave = times(wave, grown)
                along_u, before_u = advance(along_u, before_u, twice_u[half]), along_u
                along_v, before_v = advance(along_v, before_v, twice_v[half]), along_v
                grown, before_grown = advance(grown, before_grown, twice_w[half]), grown
            put_left(half, 0, k, wave[0] * along_u[0])
            put_left(half, 1, k, wave[1] * along_u[0])
            put_left(half, 2, k, wave[0] * along_u[1])
            put_left(half, 3, k, wave[1] * along_u[1])
            put_right(half, 0, k, chirp[0] * along_v[0])
            put_right(half, 1, k, chirp[1] * along_v[0])
            put_right(half, 2, k, chirp[0] * along_v[1])
            put_right(half, 3, k, chirp[1] * along_v[1])


def product(left, right, contract):
    left_high, left_low = split(left)
    right_high, right_low = split(right)
    return lax.dot_general(
        jnp.concatenate([left_high, left_high, left_low], axis=1),
        jnp.concatenate([right_high, right_low, right_high], axis=contract),
        (((1,), (contract,)), ((), ())),
        preferred_element_type=jnp.float32,
    )


def accumulate(label_ref, scale_ref, x_ref, left, right, sums):
    step = pl.program_id(0)
    part = GROUP // 2
    sources = x_ref.shape[0]
    low = lax.broadcasted_iota(jnp.int32, (GROUP, ROWS), 0) < part

    def factors(source, ch):
        def field(index):
            return x_ref[source, index * GROUP : (index + 1) * GROUP, :]

        def put(ref, half, kind, k, value):
            ref[source, ch, half, pl.ds(kind * HALF * part + k * GROUP, GROUP), :] = value

        chosen = [field(index) for index in (0, 1, 2, 3 + 2 * ch, 4 + 2 * ch)]
        factor_rows(
            chosen, scale_ref[ch], low, functools.partial(put, left), functools.partial(put, right)
        )

    def gather(source, ch):
        for slot in range(GROUP):
            label = jnp.maximum(label_ref[(step * sources + source) * GROUP + slot], 0)
            rows = pl.ds(slot % part, TERMS, stride=part)
            half = slot // part
            sums[ch, label] += product(
                left[source, ch, half, rows, :], right[source, ch, half, rows, :], 1
            )

    live = functools.reduce(
        jnp.logical_or,
        [label_ref[(step * sources + source) * GROUP] >= 0 for source in range(sources)],
    )

    @pl.when(live)
    def _():
        units = [(source, ch) for source in range(sources) for ch in range(CH)]
        factors(*units[0])
        for before, unit in zip(units[:-1], units[1:]):
            factors(*unit)
            gather(*before)
        gather(*units[-1])


def first_kernel(label_ref, scale_ref, x_ref, sums, left, right):
    @pl.when(pl.program_id(0) == 0)
    def _():
        sums[...] = jnp.zeros_like(sums)

    accumulate(label_ref, scale_ref, x_ref, left, right, sums)


def last_kernel(
    label_ref,
    scale_ref,
    corner_ref,
    tile_ref,
    x_ref,
    prior_ref,
    mix_ref,
    spread_ref,
    out_ref,
    left,
    right,
    sums,
    mixed,
    wide,
    strip,
):
    tiles = out_ref.shape[0]

    @pl.when(pl.program_id(0) == 0)
    def _():
        sums[...] = prior_ref[...]

    accumulate(label_ref, scale_ref, x_ref, left, right, sums)

    @pl.when(pl.program_id(0) == pl.num_programs(0) - 1)
    def _():
        strip[...] = jnp.zeros_like(strip)
        for ch in range(CH):
            for subgrid in range(SUBW):
                mixed[ch, subgrid * 2 * SUB : (subgrid + 1) * 2 * SUB, :] = product(
                    mix_ref[...], sums[ch, subgrid], 0
                )
            wide[ch] = product(mixed[ch], spread_ref[...], 0)
            for subgrid in range(SUBW):
                shift = corner_ref[subgrid, 1]
                rows = pl.ds(corner_ref[subgrid, 0], SUB)
                top = pl.ds(subgrid * 2 * SUB, SUB)
                bottom = pl.ds(subgrid * 2 * SUB + SUB, SUB)
                real = wide[ch, top, :GCW] - wide[ch, bottom, GCW:]
                imag = wide[ch, top, GCW:] + wide[ch, bottom, :GCW]
                strip[2 * ch, rows, :] += pltpu.roll(real, shift, 1)
                strip[2 * ch + 1, rows, :] += pltpu.roll(imag, shift, 1)
        for distance in range(tiles):
            tile = lax.rem(tile_ref[0] + distance, tiles)
            rows = pl.ds(pl.multiple_of(tile * TR, TR), TR)
            for plane in range(2 * CH):
                out_ref[distance, plane] = strip[plane, rows, :]


def transform_tables():
    k = np.arange(SUB)[:, None]
    h = np.arange(HALF)[None, :]

    def tapered(x):
        return np.sin(np.pi * (x + 0.5) / SUB) ** 2 * np.exp(-2j * np.pi * k * x / SUB)

    upper, lower = tapered(HALF + h), tapered(HALF - 1 - h)
    even, odd = upper + lower, upper - lower
    table = np.concatenate([even, 1j * even, 1j * odd, -odd], axis=1)
    real, imag = table.real, table.imag
    mix = np.concatenate([real, imag], axis=0) / (ROWS * SUB)
    spread = np.zeros((TERMS, 2 * GCW))
    spread[:, :SUB] = real.T
    spread[:, GCW : GCW + SUB] = imag.T
    return mix.astype(np.float32), spread.astype(np.float32)


SUMS = (CH, SUBW, TERMS, TERMS)
ROOM = (SPAN, CH, 2, TERMS * GROUP // 2, ROWS)


def chunk_call(kernel, prefetched, arrived, extra, out_shape, scratch):
    sources = arrived.shape[0]
    whole = [pl.BlockSpec(x.shape, lambda i, *_, n=x.ndim: (0,) * n) for x in extra]
    return pl.pallas_call(
        kernel,
        out_shape=jax.ShapeDtypeStruct(out_shape, jnp.float32),
        grid_spec=pltpu.PrefetchScalarGridSpec(
            num_scalar_prefetch=len(prefetched),
            grid=(sources // SPAN,),
            in_specs=[pl.BlockSpec((SPAN, arrived.shape[1], ROWS), lambda i, *_: (i, 0, 0))]
            + whole,
            out_specs=pl.BlockSpec(out_shape, lambda i, *_: (0,) * len(out_shape)),
            scratch_shapes=[pltpu.VMEM(shape, jnp.float32) for shape in [ROOM, ROOM] + scratch],
        ),
        compiler_params=pltpu.CompilerParams(
            dimension_semantics=("arbitrary",), vmem_limit_bytes=36 << 20
        ),
        cost_estimate=pl.CostEstimate(
            flops=3 * 2 * CH * sources * GROUP * TERMS * TERMS * ROWS,
            bytes_accessed=4 * (arrived.size + math.prod(out_shape)),
            transcendentals=0,
        ),
    )(*prefetched, arrived, *extra)


def summed_around(parts, axis):
    size = lax.axis_size(axis)
    far = size // 2
    up = [(i, (i + 1) % size) for i in range(size)]
    down = [(i, (i - 1) % size) for i in range(size)]
    rising = lax.ppermute(parts[far, :CH], axis, up)
    falling = lax.ppermute(parts[far, CH:], axis, down)
    for distance in range(far - 1, 0, -1):
        near, opposite = parts[distance], parts[size - distance]
        if distance == far - 1:
            rising = jnp.concatenate([near[:CH] + rising, near[CH:]])
            falling = jnp.concatenate([opposite[:CH], opposite[CH:] + falling])
        else:
            rising, falling = near + rising, opposite + falling
        rising = lax.ppermute(rising, axis, up)
        falling = lax.ppermute(falling, axis, down)
    return parts[0] + rising + falling


def local(block_coords, block_visibilities, subgrid_of_block, live_blocks, corners, channel_scale):
    workers = lax.axis_size("work")
    tiles = lax.axis_size("tile")
    worker = lax.axis_index("work")
    coords = jnp.swapaxes(block_coords, 0, 1)
    local_corners = lax.dynamic_slice_in_dim(corners, worker * SUBW, SUBW, 0)
    local_corners = local_corners - jnp.stack([0 * worker, worker * GCW])[None, :]
    sums = None
    for chunk in range(CHUNKS):
        packed = pack(
            chunk, subgrid_of_block, live_blocks, coords, block_visibilities, workers
        )
        arrived = lax.all_to_all(packed, "work", split_axis=0, concat_axis=0, tiled=True)
        labels = arrived[:, FIELDS * GROUP, :GROUP].astype(jnp.int32).reshape(workers * GROUP) - 1
        if chunk == 0:
            sums = chunk_call(first_kernel, (labels, channel_scale), arrived, (), SUMS, [])
    mix, spread = transform_tables()
    tile = lax.axis_index("tile").astype(jnp.int32).reshape(1)
    parts = chunk_call(
        last_kernel,
        (labels, channel_scale, local_corners, tile),
        arrived,
        (sums, jnp.asarray(mix), jnp.asarray(spread)),
        (tiles, 2 * CH, TR, GCW),
        [
            SUMS,
            (CH, SUBW * 2 * SUB, TERMS),
            (CH, SUBW * 2 * SUB, 2 * GCW),
            (2 * CH, TR * tiles, GCW),
        ],
    )
    return summed_around(parts, "tile")


def solution(mesh):
    return jax.shard_map(
        local,
        mesh=mesh,
        in_specs=(
            P(("work", "tile"), None, None),
            P(("work", "tile"), None, None),
            P(("work", "tile")),
            P(("work", "tile")),
            P(),
            P(),
        ),
        out_specs=P(None, "tile", "work"),
        check_vma=False,
    )
```

```python
import functools
import math

import jax
import jax.numpy as jnp
import numpy as np
from jax import lax
from jax.experimental import pallas as pl
from jax.experimental.pallas import tpu as pltpu
from jax.sharding import PartitionSpec as P


CH = 2
SUB = 32
HALF = SUB // 2
ROWS = 128
TR = 64
GCW = 128
SUBW = 16
FIELDS = 3 + 2 * CH
TERMS = 4 * HALF
GROUP = 8
SPAN = 8
CHUNKS = SUBW // GROUP
UNROLL = 8


def pack_kernel(chunk, label_ref, live_ref, coords_ref, waves_ref, out_ref, room, count_ref):
    workers = out_ref.shape[0]
    room[...] = jnp.zeros_like(room)

    def clear(worker, carry):
        count_ref[worker] = 0
        return carry

    lax.fori_loop(0, workers, clear, 0)
    lane = lax.broadcasted_iota(jnp.int32, (1, ROWS), 1)
    live = live_ref[0]

    def move(group, carry):
        for offset in range(UNROLL):
            block = group * UNROLL + offset
            label = label_ref[block]
            worker = label >> (SUBW.bit_length() - 1)
            count = count_ref[worker]
            count_ref[worker] = count + 1
            inside = ((count >> (GROUP.bit_length() - 1)) == chunk) & (block < live)
            place = jnp.where(inside, worker, workers)
            slot = count & (GROUP - 1)
            for field in range(FIELDS):
                if field < 3:
                    value = coords_ref[field, pl.ds(block, 1), :]
                else:
                    value = waves_ref[block, pl.ds(field - 3, 1), :]
                room[place, pl.ds(field * GROUP + slot, 1), :] = value
            row = pl.ds(FIELDS * GROUP, 1)
            mark = ((label & (SUBW - 1)) + 1).astype(jnp.float32)
            room[place, row, :] = jnp.where(lane == slot, mark, room[place, row, :])
        return carry

    lax.fori_loop(0, label_ref.shape[0] // UNROLL, move, 0)
    out_ref[...] = room[:workers]


def pack(chunk, labels, live, coords, waves, workers):
    smem = pl.BlockSpec(memory_space=pltpu.SMEM)
    vmem = pl.BlockSpec(memory_space=pltpu.VMEM)
    shape = (workers, (FIELDS + 1) * GROUP, ROWS)
    return pl.pallas_call(
        functools.partial(pack_kernel, chunk),
        name="pack",
        out_shape=jax.ShapeDtypeStruct(shape, jnp.float32),
        in_specs=[smem, smem, vmem, vmem],
        out_specs=vmem,
        scratch_shapes=[
            pltpu.VMEM((workers + 1,) + shape[1:], jnp.float32),
            pltpu.SMEM((workers,), jnp.int32),
        ],
        cost_estimate=pl.CostEstimate(
            flops=0, bytes_accessed=4 * math.prod(shape), transcendentals=0
        ),
    )(labels, live, coords, waves)


def series(square, first, count):
    terms = [(-1.0) ** n / math.factorial(2 * n + first) for n in range(count)]
    total = square * terms[-1] + terms[-2]
    for term in terms[-3::-1]:
        total = total * square + term
    return total


def sin_cos(theta, sin_terms, cos_terms):
    square = theta * theta
    return series(square, 0, cos_terms), series(square, 1, sin_terms) * theta


def times(a, b):
    return a[0] * b[0] - a[1] * b[1], a[0] * b[1] + a[1] * b[0]


def split(value):
    high = value.astype(jnp.bfloat16)
    low = (value - high.astype(jnp.float32)).astype(jnp.bfloat16)
    return high, low


def advance(current, previous, twice_sine):
    return (
        previous[0] - twice_sine * current[1],
        previous[1] + twice_sine * current[0],
    )


def exchange(value):
    return pltpu.roll(value, GROUP // 2, 0)


def interleave(even, odd, low):
    return (
        jnp.where(low, even, exchange(odd)),
        jnp.where(low, exchange(even), odd),
    )


def interleave_pair(even, odd, low):
    real, imag = interleave(even[0], odd[0], low), interleave(even[1], odd[1], low)
    return (real[0], imag[0]), (real[1], imag[1])


def factor_rows(fields, factor, low, put_left, put_right):
    u, v, w = fields[:3]
    first = u * (factor * (2.0 * math.pi / (2 * SUB)))
    second = v * (factor * (2.0 * math.pi / (2 * SUB)))
    depth = w * (factor * (math.pi / (SUB * SUB)))
    along_u = sin_cos(first - depth, 5, 5)
    along_v = sin_cos(second - depth, 5, 5)
    turn = sin_cos(depth * 4.0, 3, 3)
    whole_u, whole_v = times(along_u, along_u), times(along_v, along_v)
    turn2 = times(turn, turn)
    turn3 = times(turn2, turn)
    both = times(along_u, along_v)
    wave = times(fields[3:], (both[0], -both[1]))
    one, zero = jnp.ones_like(u), jnp.zeros_like(u)
    all_u = interleave_pair(along_u, times(whole_u, along_u), low)
    all_v = interleave_pair(along_v, times(whole_v, along_v), low)
    all_wave = interleave_pair(wave, times(wave, turn), low)
    all_chirp = interleave_pair((one, zero), turn, low)
    all_grown = interleave_pair(turn3, times(turn3, turn2), low)
    all_before = interleave_pair((turn[0], -turn[1]), turn, low)
    twice_u = interleave(*[whole_u[0] * whole_u[1] * 4.0] * 2, low)
    twice_v = interleave(*[whole_v[0] * whole_v[1] * 4.0] * 2, low)
    twice_w = interleave(*[turn2[0] * turn2[1] * 4.0] * 2, low)
    for half in range(2):
        along_u, along_v = all_u[half], all_v[half]
        wave, chirp = all_wave[half], all_chirp[half]
        grown, before_grown = all_grown[half], all_before[half]
        before_u = (exchange(along_u[0]), -exchange(along_u[1]))
        before_v = (exchange(along_v[0]), -exchange(along_v[1]))
        for k in range(HALF // 2):
            if k > 0:
                chirp = times(chirp, grown)
                wave = times(wave, grown)
                along_u, before_u = advance(along_u, before_u, twice_u[half]), along_u
                along_v, before_v = advance(along_v, before_v, twice_v[half]), along_v
                grown, before_grown = advance(grown, before_grown, twice_w[half]), grown
            put_left(half, 0, k, wave[0] * along_u[0])
            put_left(half, 1, k, wave[1] * along_u[0])
            put_left(half, 2, k, wave[0] * along_u[1])
            put_left(half, 3, k, wave[1] * along_u[1])
            put_right(half, 0, k, chirp[0] * along_v[0])
            put_right(half, 1, k, chirp[1] * along_v[0])
            put_right(half, 2, k, chirp[0] * along_v[1])
            put_right(half, 3, k, chirp[1] * along_v[1])


def product(left, right, contract):
    left_high, left_low = split(left)
    right_high, right_low = split(right)
    return lax.dot_general(
        jnp.concatenate([left_high, left_high, left_low], axis=1),
        jnp.concatenate([right_high, right_low, right_high], axis=contract),
        (((1,), (contract,)), ((), ())),
        preferred_element_type=jnp.float32,
    )


def accumulate(label_ref, scale_ref, x_ref, left, right, sums):
    step = pl.program_id(0)
    part = GROUP // 2
    sources = x_ref.shape[0]
    low = lax.broadcasted_iota(jnp.int32, (GROUP, ROWS), 0) < part

    def factors(source, ch):
        def field(index):
            return x_ref[source, index * GROUP : (index + 1) * GROUP, :]

        def put(ref, half, kind, k, value):
            ref[source, ch, half, pl.ds(kind * HALF * part + k * GROUP, GROUP), :] = value

        chosen = [field(index) for index in (0, 1, 2, 3 + 2 * ch, 4 + 2 * ch)]
        factor_rows(
            chosen, scale_ref[ch], low, functools.partial(put, left), functools.partial(put, right)
        )

    def gather(source, ch):
        for slot in range(GROUP):
            label = jnp.maximum(label_ref[(step * sources + source) * GROUP + slot], 0)
            rows = pl.ds(slot % part, TERMS, stride=part)
            half = slot // part
            sums[ch, label] += product(
                left[source, ch, half, rows, :], right[source, ch, half, rows, :], 1
            )

    live = functools.reduce(
        jnp.logical_or,
        [label_ref[(step * sources + source) * GROUP] >= 0 for source in range(sources)],
    )

    @pl.when(live)
    def _():
        units = [(source, ch) for source in range(sources) for ch in range(CH)]
        factors(*units[0])
        for before, unit in zip(units[:-1], units[1:]):
            factors(*unit)
            gather(*before)
        gather(*units[-1])


def first_kernel(label_ref, scale_ref, x_ref, sums, left, right):
    @pl.when(pl.program_id(0) == 0)
    def _():
        sums[...] = jnp.zeros_like(sums)

    accumulate(label_ref, scale_ref, x_ref, left, right, sums)


def last_kernel(
    label_ref,
    scale_ref,
    corner_ref,
    tile_ref,
    x_ref,
    prior_ref,
    mix_ref,
    spread_ref,
    out_ref,
    left,
    right,
    sums,
    mixed,
    wide,
    strip,
):
    tiles = out_ref.shape[0]

    @pl.when(pl.program_id(0) == 0)
    def _():
        sums[...] = prior_ref[...]

    accumulate(label_ref, scale_ref, x_ref, left, right, sums)

    @pl.when(pl.program_id(0) == pl.num_programs(0) - 1)
    def _():
        strip[...] = jnp.zeros_like(strip)
        for ch in range(CH):
            for subgrid in range(SUBW):
                mixed[ch, subgrid * 2 * SUB : (subgrid + 1) * 2 * SUB, :] = product(
                    mix_ref[...], sums[ch, subgrid], 0
                )
            wide[ch] = product(mixed[ch], spread_ref[...], 0)
            for subgrid in range(SUBW):
                shift = corner_ref[subgrid, 1]
                rows = pl.ds(corner_ref[subgrid, 0], SUB)
                top = pl.ds(subgrid * 2 * SUB, SUB)
                bottom = pl.ds(subgrid * 2 * SUB + SUB, SUB)
                real = wide[ch, top, :GCW] - wide[ch, bottom, GCW:]
                imag = wide[ch, top, GCW:] + wide[ch, bottom, :GCW]
                strip[2 * ch, rows, :] += pltpu.roll(real, shift, 1)
                strip[2 * ch + 1, rows, :] += pltpu.roll(imag, shift, 1)
        for distance in range(tiles):
            tile = lax.rem(tile_ref[0] + distance, tiles)
            rows = pl.ds(pl.multiple_of(tile * TR, TR), TR)
            for plane in range(2 * CH):
                out_ref[distance, plane] = strip[plane, rows, :]


def transform_tables():
    k = np.arange(SUB)[:, None]
    h = np.arange(HALF)[None, :]

    def tapered(x):
        return np.sin(np.pi * (x + 0.5) / SUB) ** 2 * np.exp(-2j * np.pi * k * x / SUB)

    upper, lower = tapered(HALF + h), tapered(HALF - 1 - h)
    even, odd = upper + lower, upper - lower
    table = np.concatenate([even, 1j * even, 1j * odd, -odd], axis=1)
    real, imag = table.real, table.imag
    mix = np.concatenate([real, imag], axis=0) / (ROWS * SUB)
    spread = np.zeros((TERMS, 2 * GCW))
    spread[:, :SUB] = real.T
    spread[:, GCW : GCW + SUB] = imag.T
    return mix.astype(np.float32), spread.astype(np.float32)


SUMS = (CH, SUBW, TERMS, TERMS)
ROOM = (SPAN, CH, 2, TERMS * GROUP // 2, ROWS)


def chunk_call(kernel, prefetched, arrived, extra, out_shape, scratch):
    sources = arrived.shape[0]
    whole = [pl.BlockSpec(x.shape, lambda i, *_, n=x.ndim: (0,) * n) for x in extra]
    return pl.pallas_call(
        kernel,
        out_shape=jax.ShapeDtypeStruct(out_shape, jnp.float32),
        grid_spec=pltpu.PrefetchScalarGridSpec(
            num_scalar_prefetch=len(prefetched),
            grid=(sources // SPAN,),
            in_specs=[pl.BlockSpec((SPAN, arrived.shape[1], ROWS), lambda i, *_: (i, 0, 0))]
            + whole,
            out_specs=pl.BlockSpec(out_shape, lambda i, *_: (0,) * len(out_shape)),
            scratch_shapes=[pltpu.VMEM(shape, jnp.float32) for shape in [ROOM, ROOM] + scratch],
        ),
        compiler_params=pltpu.CompilerParams(
            dimension_semantics=("arbitrary",), vmem_limit_bytes=36 << 20
        ),
        cost_estimate=pl.CostEstimate(
            flops=3 * 2 * CH * sources * GROUP * TERMS * TERMS * ROWS,
            bytes_accessed=4 * (arrived.size + math.prod(out_shape)),
            transcendentals=0,
        ),
    )(*prefetched, arrived, *extra)


def summed_around(parts, axis):
    size = lax.axis_size(axis)
    far = size // 2
    up = [(i, (i + 1) % size) for i in range(size)]
    down = [(i, (i - 1) % size) for i in range(size)]
    rising = lax.ppermute(parts[far, :CH], axis, up)
    falling = lax.ppermute(parts[far, CH:], axis, down)
    for distance in range(far - 1, 0, -1):
        near, opposite = parts[distance], parts[size - distance]
        if distance == far - 1:
            rising = jnp.concatenate([near[:CH] + rising, near[CH:]])
            falling = jnp.concatenate([opposite[:CH], opposite[CH:] + falling])
        else:
            rising, falling = near + rising, opposite + falling
        rising = lax.ppermute(rising, axis, up)
        falling = lax.ppermute(falling, axis, down)
    return parts[0] + rising + falling


def local(block_coords, block_visibilities, subgrid_of_block, live_blocks, corners, channel_scale):
    workers = lax.axis_size("work")
    tiles = lax.axis_size("tile")
    worker = lax.axis_index("work")
    coords = jnp.swapaxes(block_coords, 0, 1)
    local_corners = lax.dynamic_slice_in_dim(corners, worker * SUBW, SUBW, 0)
    local_corners = local_corners - jnp.stack([0 * worker, worker * GCW])[None, :]
    sums = None
    for chunk in range(CHUNKS):
        packed = pack(
            chunk, subgrid_of_block, live_blocks, coords, block_visibilities, workers
        )
        arrived = lax.all_to_all(packed, "work", split_axis=0, concat_axis=0, tiled=True)
        labels = arrived[:, FIELDS * GROUP, :GROUP].astype(jnp.int32).reshape(workers * GROUP) - 1
        if chunk == 0:
            sums = chunk_call(first_kernel, (labels, channel_scale), arrived, (), SUMS, [])
    mix, spread = transform_tables()
    tile = lax.axis_index("tile").astype(jnp.int32).reshape(1)
    parts = chunk_call(
        last_kernel,
        (labels, channel_scale, local_corners, tile),
        arrived,
        (sums, jnp.asarray(mix), jnp.asarray(spread)),
        (tiles, 2 * CH, TR, GCW),
        [
            SUMS,
            (CH, SUBW * 2 * SUB, TERMS),
            (CH, SUBW * 2 * SUB, 2 * GCW),
            (2 * CH, TR * tiles, GCW),
        ],
    )
    return summed_around(parts, "tile")


def solution(mesh):
    return jax.shard_map(
        local,
        mesh=mesh,
        in_specs=(
            P(("work", "tile"), None, None),
            P(("work", "tile"), None, None),
            P(("work", "tile")),
            P(("work", "tile")),
            P(),
            P(),
        ),
        out_specs=P(None, "tile", "work"),
        check_vma=False,
    )
```

```python
import functools
import math

import jax
import jax.numpy as jnp
import numpy as np
from jax import lax
from jax.experimental import pallas as pl
from jax.experimental.pallas import tpu as pltpu
from jax.sharding import PartitionSpec as P


CH = 2
SUB = 32
HALF = SUB // 2
ROWS = 128
TR = 64
GCW = 128
SUBW = 16
FIELDS = 3 + 2 * CH
TERMS = 4 * HALF
GROUP = 8
SPAN = 8
CHUNKS = SUBW // GROUP
UNROLL = 8


def pack_kernel(chunk, label_ref, live_ref, coords_ref, waves_ref, out_ref, room, count_ref):
    workers = out_ref.shape[0]
    room[...] = jnp.zeros_like(room)

    def clear(worker, carry):
        count_ref[worker] = 0
        return carry

    lax.fori_loop(0, workers, clear, 0)
    lane = lax.broadcasted_iota(jnp.int32, (1, ROWS), 1)
    live = live_ref[0]

    def move(group, carry):
        for offset in range(UNROLL):
            block = group * UNROLL + offset
            label = label_ref[block]
            worker = label >> (SUBW.bit_length() - 1)
            count = count_ref[worker]
            count_ref[worker] = count + 1
            inside = ((count >> (GROUP.bit_length() - 1)) == chunk) & (block < live)
            place = jnp.where(inside, worker, workers)
            slot = count & (GROUP - 1)
            for field in range(FIELDS):
                if field < 3:
                    value = coords_ref[field, pl.ds(block, 1), :]
                else:
                    value = waves_ref[block, pl.ds(field - 3, 1), :]
                room[place, pl.ds(field * GROUP + slot, 1), :] = value
            row = pl.ds(FIELDS * GROUP, 1)
            mark = ((label & (SUBW - 1)) + 1).astype(jnp.float32)
            room[place, row, :] = jnp.where(lane == slot, mark, room[place, row, :])
        return carry

    lax.fori_loop(0, label_ref.shape[0] // UNROLL, move, 0)
    out_ref[...] = room[:workers]


def pack(chunk, labels, live, coords, waves, workers):
    smem = pl.BlockSpec(memory_space=pltpu.SMEM)
    vmem = pl.BlockSpec(memory_space=pltpu.VMEM)
    shape = (workers, (FIELDS + 1) * GROUP, ROWS)
    return pl.pallas_call(
        functools.partial(pack_kernel, chunk),
        name="pack",
        out_shape=jax.ShapeDtypeStruct(shape, jnp.float32),
        in_specs=[smem, smem, vmem, vmem],
        out_specs=vmem,
        scratch_shapes=[
            pltpu.VMEM((workers + 1,) + shape[1:], jnp.float32),
            pltpu.SMEM((workers,), jnp.int32),
        ],
        cost_estimate=pl.CostEstimate(
            flops=0, bytes_accessed=4 * math.prod(shape), transcendentals=0
        ),
    )(labels, live, coords, waves)


def series(square, first, count):
    terms = [(-1.0) ** n / math.factorial(2 * n + first) for n in range(count)]
    total = square * terms[-1] + terms[-2]
    for term in terms[-3::-1]:
        total = total * square + term
    return total


def sin_cos(theta, sin_terms, cos_terms):
    square = theta * theta
    return series(square, 0, cos_terms), series(square, 1, sin_terms) * theta


def times(a, b):
    return a[0] * b[0] - a[1] * b[1], a[0] * b[1] + a[1] * b[0]


def split(value):
    high = value.astype(jnp.bfloat16)
    low = (value - high.astype(jnp.float32)).astype(jnp.bfloat16)
    return high, low


def advance(current, previous, twice_sine):
    return (
        previous[0] - twice_sine * current[1],
        previous[1] + twice_sine * current[0],
    )


def exchange(value):
    return pltpu.roll(value, GROUP // 2, 0)


def interleave(even, odd, low):
    return (
        jnp.where(low, even, exchange(odd)),
        jnp.where(low, exchange(even), odd),
    )


def interleave_pair(even, odd, low):
    real, imag = interleave(even[0], odd[0], low), interleave(even[1], odd[1], low)
    return (real[0], imag[0]), (real[1], imag[1])


def factor_rows(fields, factor, low, put_left, put_right):
    u, v, w = fields[:3]
    first = u * (factor * (2.0 * math.pi / (2 * SUB)))
    second = v * (factor * (2.0 * math.pi / (2 * SUB)))
    depth = w * (factor * (math.pi / (SUB * SUB)))
    along_u = sin_cos(first - depth, 5, 5)
    along_v = sin_cos(second - depth, 5, 5)
    turn = sin_cos(depth * 4.0, 3, 3)
    whole_u, whole_v = times(along_u, along_u), times(along_v, along_v)
    turn2 = times(turn, turn)
    turn3 = times(turn2, turn)
    both = times(along_u, along_v)
    wave = times(fields[3:], (both[0], -both[1]))
    one, zero = jnp.ones_like(u), jnp.zeros_like(u)
    all_u = interleave_pair(along_u, times(whole_u, along_u), low)
    all_v = interleave_pair(along_v, times(whole_v, along_v), low)
    all_wave = interleave_pair(wave, times(wave, turn), low)
    all_chirp = interleave_pair((one, zero), turn, low)
    all_grown = interleave_pair(turn3, times(turn3, turn2), low)
    all_before = interleave_pair((turn[0], -turn[1]), turn, low)
    twice_u = interleave(*[whole_u[0] * whole_u[1] * 4.0] * 2, low)
    twice_v = interleave(*[whole_v[0] * whole_v[1] * 4.0] * 2, low)
    twice_w = interleave(*[turn2[0] * turn2[1] * 4.0] * 2, low)
    for half in range(2):
        along_u, along_v = all_u[half], all_v[half]
        wave, chirp = all_wave[half], all_chirp[half]
        grown, before_grown = all_grown[half], all_before[half]
        before_u = (exchange(along_u[0]), -exchange(along_u[1]))
        before_v = (exchange(along_v[0]), -exchange(along_v[1]))
        for k in range(HALF // 2):
            if k > 0:
                chirp = times(chirp, grown)
                wave = times(wave, grown)
                along_u, before_u = advance(along_u, before_u, twice_u[half]), along_u
                along_v, before_v = advance(along_v, before_v, twice_v[half]), along_v
                grown, before_grown = advance(grown, before_grown, twice_w[half]), grown
            put_left(half, 0, k, wave[0] * along_u[0])
            put_left(half, 1, k, wave[1] * along_u[0])
            put_left(half, 2, k, wave[0] * along_u[1])
            put_left(half, 3, k, wave[1] * along_u[1])
            put_right(half, 0, k, chirp[0] * along_v[0])
            put_right(half, 1, k, chirp[1] * along_v[0])
            put_right(half, 2, k, chirp[0] * along_v[1])
            put_right(half, 3, k, chirp[1] * along_v[1])


def product(left, right, contract):
    left_high, left_low = split(left)
    right_high, right_low = split(right)
    return lax.dot_general(
        jnp.concatenate([left_high, left_high, left_low], axis=1),
        jnp.concatenate([right_high, right_low, right_high], axis=contract),
        (((1,), (contract,)), ((), ())),
        preferred_element_type=jnp.float32,
    )


def accumulate(label_ref, scale_ref, x_ref, left, right, sums):
    step = pl.program_id(0)
    part = GROUP // 2
    sources = x_ref.shape[0]
    low = lax.broadcasted_iota(jnp.int32, (GROUP, ROWS), 0) < part

    def factors(source, ch):
        def field(index):
            return x_ref[source, index * GROUP : (index + 1) * GROUP, :]

        def put(ref, half, kind, k, value):
            ref[source, ch, half, pl.ds(kind * HALF * part + k * GROUP, GROUP), :] = value

        chosen = [field(index) for index in (0, 1, 2, 3 + 2 * ch, 4 + 2 * ch)]
        factor_rows(
            chosen, scale_ref[ch], low, functools.partial(put, left), functools.partial(put, right)
        )

    def gather(source, ch):
        for slot in range(GROUP):
            label = jnp.maximum(label_ref[(step * sources + source) * GROUP + slot], 0)
            rows = pl.ds(slot % part, TERMS, stride=part)
            half = slot // part
            sums[ch, label] += product(
                left[source, ch, half, rows, :], right[source, ch, half, rows, :], 1
            )

    live = functools.reduce(
        jnp.logical_or,
        [label_ref[(step * sources + source) * GROUP] >= 0 for source in range(sources)],
    )

    @pl.when(live)
    def _():
        units = [(source, ch) for source in range(sources) for ch in range(CH)]
        factors(*units[0])
        for before, unit in zip(units[:-1], units[1:]):
            factors(*unit)
            gather(*before)
        gather(*units[-1])


def first_kernel(label_ref, scale_ref, x_ref, sums, left, right):
    @pl.when(pl.program_id(0) == 0)
    def _():
        sums[...] = jnp.zeros_like(sums)

    accumulate(label_ref, scale_ref, x_ref, left, right, sums)


def last_kernel(
    label_ref,
    scale_ref,
    corner_ref,
    tile_ref,
    x_ref,
    prior_ref,
    mix_ref,
    spread_ref,
    out_ref,
    left,
    right,
    sums,
    mixed,
    wide,
    strip,
):
    tiles = out_ref.shape[0]

    @pl.when(pl.program_id(0) == 0)
    def _():
        sums[...] = prior_ref[...]

    accumulate(label_ref, scale_ref, x_ref, left, right, sums)

    @pl.when(pl.program_id(0) == pl.num_programs(0) - 1)
    def _():
        strip[...] = jnp.zeros_like(strip)
        for ch in range(CH):
            for subgrid in range(SUBW):
                mixed[ch, subgrid * 2 * SUB : (subgrid + 1) * 2 * SUB, :] = product(
                    mix_ref[...], sums[ch, subgrid], 0
                )
            wide[ch] = product(mixed[ch], spread_ref[...], 0)
            for subgrid in range(SUBW):
                shift = corner_ref[subgrid, 1]
                rows = pl.ds(corner_ref[subgrid, 0], SUB)
                top = pl.ds(subgrid * 2 * SUB, SUB)
                bottom = pl.ds(subgrid * 2 * SUB + SUB, SUB)
                real = wide[ch, top, :GCW] - wide[ch, bottom, GCW:]
                imag = wide[ch, top, GCW:] + wide[ch, bottom, :GCW]
                strip[2 * ch, rows, :] += pltpu.roll(real, shift, 1)
                strip[2 * ch + 1, rows, :] += pltpu.roll(imag, shift, 1)
        for distance in range(tiles):
            tile = lax.rem(tile_ref[0] + distance, tiles)
            rows = pl.ds(pl.multiple_of(tile * TR, TR), TR)
            for plane in range(2 * CH):
                out_ref[distance, plane] = strip[plane, rows, :]


def transform_tables():
    k = np.arange(SUB)[:, None]
    h = np.arange(HALF)[None, :]

    def tapered(x):
        return np.sin(np.pi * (x + 0.5) / SUB) ** 2 * np.exp(-2j * np.pi * k * x / SUB)

    upper, lower = tapered(HALF + h), tapered(HALF - 1 - h)
    even, odd = upper + lower, upper - lower
    table = np.concatenate([even, 1j * even, 1j * odd, -odd], axis=1)
    real, imag = table.real, table.imag
    mix = np.concatenate([real, imag], axis=0) / (ROWS * SUB)
    spread = np.zeros((TERMS, 2 * GCW))
    spread[:, :SUB] = real.T
    spread[:, GCW : GCW + SUB] = imag.T
    return mix.astype(np.float32), spread.astype(np.float32)


SUMS = (CH, SUBW, TERMS, TERMS)
ROOM = (SPAN, CH, 2, TERMS * GROUP // 2, ROWS)


def chunk_call(kernel, prefetched, arrived, extra, out_shape, scratch):
    sources = arrived.shape[0]
    whole = [pl.BlockSpec(x.shape, lambda i, *_, n=x.ndim: (0,) * n) for x in extra]
    return pl.pallas_call(
        kernel,
        out_shape=jax.ShapeDtypeStruct(out_shape, jnp.float32),
        grid_spec=pltpu.PrefetchScalarGridSpec(
            num_scalar_prefetch=len(prefetched),
            grid=(sources // SPAN,),
            in_specs=[pl.BlockSpec((SPAN, arrived.shape[1], ROWS), lambda i, *_: (i, 0, 0))]
            + whole,
            out_specs=pl.BlockSpec(out_shape, lambda i, *_: (0,) * len(out_shape)),
            scratch_shapes=[pltpu.VMEM(shape, jnp.float32) for shape in [ROOM, ROOM] + scratch],
        ),
        compiler_params=pltpu.CompilerParams(
            dimension_semantics=("arbitrary",), vmem_limit_bytes=36 << 20
        ),
        cost_estimate=pl.CostEstimate(
            flops=3 * 2 * CH * sources * GROUP * TERMS * TERMS * ROWS,
            bytes_accessed=4 * (arrived.size + math.prod(out_shape)),
            transcendentals=0,
        ),
    )(*prefetched, arrived, *extra)


def summed_around(parts, axis):
    size = lax.axis_size(axis)

    def sent(value, hops):
        return lax.ppermute(value, axis, [(i, (i + hops) % size) for i in range(size)])

    rising = sent(jnp.concatenate([parts[3], parts[4, :CH]]), 2)
    falling = sent(jnp.concatenate([parts[5], parts[4, CH:]]), -2)
    planes = 2 * CH
    pieces = [
        sent(jnp.concatenate([parts[2, :CH] + rising[planes:], parts[2, CH:]]), 2),
        sent(jnp.concatenate([parts[6, :CH], parts[6, CH:] + falling[planes:]]), -2),
        sent(parts[1] + rising[:planes], 1),
        sent(parts[7] + falling[:planes], -1),
    ]
    return sum(pieces, parts[0])


def local(block_coords, block_visibilities, subgrid_of_block, live_blocks, corners, channel_scale):
    workers = lax.axis_size("work")
    tiles = lax.axis_size("tile")
    worker = lax.axis_index("work")
    coords = jnp.swapaxes(block_coords, 0, 1)
    local_corners = lax.dynamic_slice_in_dim(corners, worker * SUBW, SUBW, 0)
    local_corners = local_corners - jnp.stack([0 * worker, worker * GCW])[None, :]
    sums = None
    for chunk in range(CHUNKS):
        packed = pack(
            chunk, subgrid_of_block, live_blocks, coords, block_visibilities, workers
        )
        arrived = lax.all_to_all(packed, "work", split_axis=0, concat_axis=0, tiled=True)
        labels = arrived[:, FIELDS * GROUP, :GROUP].astype(jnp.int32).reshape(workers * GROUP) - 1
        if chunk == 0:
            sums = chunk_call(first_kernel, (labels, channel_scale), arrived, (), SUMS, [])
    mix, spread = transform_tables()
    tile = lax.axis_index("tile").astype(jnp.int32).reshape(1)
    parts = chunk_call(
        last_kernel,
        (labels, channel_scale, local_corners, tile),
        arrived,
        (sums, jnp.asarray(mix), jnp.asarray(spread)),
        (tiles, 2 * CH, TR, GCW),
        [
            SUMS,
            (CH, SUBW * 2 * SUB, TERMS),
            (CH, SUBW * 2 * SUB, 2 * GCW),
            (2 * CH, TR * tiles, GCW),
        ],
    )
    return summed_around(parts, "tile")


def solution(mesh):
    return jax.shard_map(
        local,
        mesh=mesh,
        in_specs=(
            P(("work", "tile"), None, None),
            P(("work", "tile"), None, None),
            P(("work", "tile")),
            P(("work", "tile")),
            P(),
            P(),
        ),
        out_specs=P(None, "tile", "work"),
        check_vma=False,
    )
```

```python
import functools
import math

import jax
import jax.numpy as jnp
import numpy as np
from jax import lax
from jax.experimental import pallas as pl
from jax.experimental.pallas import tpu as pltpu
from jax.sharding import PartitionSpec as P


CH = 2
SUB = 32
HALF = SUB // 2
ROWS = 128
TR = 64
GCW = 128
SUBW = 16
FIELDS = 3 + 2 * CH
TERMS = 4 * HALF
GROUP = 8
SPAN = 8
CHUNKS = SUBW // GROUP
UNROLL = 8


def pack_kernel(chunk, label_ref, live_ref, coords_ref, waves_ref, out_ref, room, count_ref):
    workers = out_ref.shape[0]
    room[...] = jnp.zeros_like(room)

    def clear(worker, carry):
        count_ref[worker] = 0
        return carry

    lax.fori_loop(0, workers, clear, 0)
    lane = lax.broadcasted_iota(jnp.int32, (1, ROWS), 1)
    live = live_ref[0]

    def move(group, carry):
        for offset in range(UNROLL):
            block = group * UNROLL + offset
            label = label_ref[block]
            worker = label >> (SUBW.bit_length() - 1)
            count = count_ref[worker]
            count_ref[worker] = count + 1
            inside = ((count >> (GROUP.bit_length() - 1)) == chunk) & (block < live)
            place = jnp.where(inside, worker, workers)
            slot = count & (GROUP - 1)
            for field in range(FIELDS):
                if field < 3:
                    value = coords_ref[field, pl.ds(block, 1), :]
                else:
                    value = waves_ref[block, pl.ds(field - 3, 1), :]
                room[place, pl.ds(field * GROUP + slot, 1), :] = value
            row = pl.ds(FIELDS * GROUP, 1)
            mark = ((label & (SUBW - 1)) + 1).astype(jnp.float32)
            room[place, row, :] = jnp.where(lane == slot, mark, room[place, row, :])
        return carry

    lax.fori_loop(0, label_ref.shape[0] // UNROLL, move, 0)
    out_ref[...] = room[:workers]


def pack(chunk, labels, live, coords, waves, workers):
    smem = pl.BlockSpec(memory_space=pltpu.SMEM)
    vmem = pl.BlockSpec(memory_space=pltpu.VMEM)
    shape = (workers, (FIELDS + 1) * GROUP, ROWS)
    return pl.pallas_call(
        functools.partial(pack_kernel, chunk),
        name="pack",
        out_shape=jax.ShapeDtypeStruct(shape, jnp.float32),
        in_specs=[smem, smem, vmem, vmem],
        out_specs=vmem,
        scratch_shapes=[
            pltpu.VMEM((workers + 1,) + shape[1:], jnp.float32),
            pltpu.SMEM((workers,), jnp.int32),
        ],
        cost_estimate=pl.CostEstimate(
            flops=0, bytes_accessed=4 * math.prod(shape), transcendentals=0
        ),
    )(labels, live, coords, waves)


def series(square, first, count):
    terms = [(-1.0) ** n / math.factorial(2 * n + first) for n in range(count)]
    total = square * terms[-1] + terms[-2]
    for term in terms[-3::-1]:
        total = total * square + term
    return total


def sin_cos(theta, sin_terms, cos_terms):
    square = theta * theta
    return series(square, 0, cos_terms), series(square, 1, sin_terms) * theta


def times(a, b):
    return a[0] * b[0] - a[1] * b[1], a[0] * b[1] + a[1] * b[0]


def split(value):
    high = value.astype(jnp.bfloat16)
    low = (value - high.astype(jnp.float32)).astype(jnp.bfloat16)
    return high, low


def advance(current, previous, twice_sine):
    return (
        previous[0] - twice_sine * current[1],
        previous[1] + twice_sine * current[0],
    )


def exchange(value):
    return pltpu.roll(value, GROUP // 2, 0)


def interleave(even, odd, low):
    return (
        jnp.where(low, even, exchange(odd)),
        jnp.where(low, exchange(even), odd),
    )


def interleave_pair(even, odd, low):
    real, imag = interleave(even[0], odd[0], low), interleave(even[1], odd[1], low)
    return (real[0], imag[0]), (real[1], imag[1])


def factor_rows(fields, factor, depth_factor, low, put_left, put_right):
    u, v, w = fields[:3]
    first = u * factor
    second = v * factor
    depth = w * depth_factor
    along_u = sin_cos(first - depth, 5, 5)
    along_v = sin_cos(second - depth, 5, 5)
    turn = sin_cos(depth * 4.0, 3, 3)
    whole_u, whole_v = times(along_u, along_u), times(along_v, along_v)
    turn2 = times(turn, turn)
    turn3 = times(turn2, turn)
    both = times(along_u, along_v)
    wave = times(fields[3:], (both[0], -both[1]))
    one, zero = jnp.ones_like(u), jnp.zeros_like(u)
    all_u = interleave_pair(along_u, times(whole_u, along_u), low)
    all_v = interleave_pair(along_v, times(whole_v, along_v), low)
    all_wave = interleave_pair(wave, times(wave, turn), low)
    all_chirp = interleave_pair((one, zero), turn, low)
    all_grown = interleave_pair(turn3, times(turn3, turn2), low)
    all_before = interleave_pair((turn[0], -turn[1]), turn, low)
    twice_u = interleave(*[whole_u[0] * whole_u[1] * 4.0] * 2, low)
    twice_v = interleave(*[whole_v[0] * whole_v[1] * 4.0] * 2, low)
    twice_w = interleave(*[turn2[0] * turn2[1] * 4.0] * 2, low)
    for half in range(2):
        along_u, along_v = all_u[half], all_v[half]
        wave, chirp = all_wave[half], all_chirp[half]
        grown, before_grown = all_grown[half], all_before[half]
        before_u = (exchange(along_u[0]), -exchange(along_u[1]))
        before_v = (exchange(along_v[0]), -exchange(along_v[1]))
        for k in range(HALF // 2):
            if k > 0:
                chirp = times(chirp, grown)
                wave = times(wave, grown)
                along_u, before_u = advance(along_u, before_u, twice_u[half]), along_u
                along_v, before_v = advance(along_v, before_v, twice_v[half]), along_v
                grown, before_grown = advance(grown, before_grown, twice_w[half]), grown
            put_left(half, 0, k, wave[0] * along_u[0])
            put_left(half, 1, k, wave[1] * along_u[0])
            put_left(half, 2, k, wave[0] * along_u[1])
            put_left(half, 3, k, wave[1] * along_u[1])
            put_right(half, 0, k, chirp[0] * along_v[0])
            put_right(half, 1, k, chirp[1] * along_v[0])
            put_right(half, 2, k, chirp[0] * along_v[1])
            put_right(half, 3, k, chirp[1] * along_v[1])


def product(left, right, contract):
    left_high, left_low = split(left)
    right_high, right_low = split(right)
    return lax.dot_general(
        jnp.concatenate([left_high, left_high, left_low], axis=1),
        jnp.concatenate([right_high, right_low, right_high], axis=contract),
        (((1,), (contract,)), ((), ())),
        preferred_element_type=jnp.float32,
    )


def accumulate(label_ref, scale_ref, x_ref, left, right, sums):
    step = pl.program_id(0)
    part = GROUP // 2
    sources = x_ref.shape[0]
    low = lax.broadcasted_iota(jnp.int32, (GROUP, ROWS), 0) < part

    def factors(source, ch):
        def field(index):
            return x_ref[source, index * GROUP : (index + 1) * GROUP, :]

        def put(ref, half, kind, k, value):
            ref[source, ch, half, pl.ds(kind * HALF * part + k * GROUP, GROUP), :] = value

        chosen = [field(index) for index in (0, 1, 2, 3 + 2 * ch, 4 + 2 * ch)]
        factor_rows(
            chosen,
            scale_ref[ch],
            scale_ref[CH + ch],
            low,
            functools.partial(put, left),
            functools.partial(put, right),
        )

    def gather(source, ch):
        for slot in range(GROUP):
            label = jnp.maximum(label_ref[(step * sources + source) * GROUP + slot], 0)
            rows = pl.ds(slot % part, TERMS, stride=part)
            half = slot // part
            sums[ch, label] += product(
                left[source, ch, half, rows, :], right[source, ch, half, rows, :], 1
            )

    live = functools.reduce(
        jnp.logical_or,
        [label_ref[(step * sources + source) * GROUP] >= 0 for source in range(sources)],
    )

    @pl.when(live)
    def _():
        units = [(source, ch) for source in range(sources) for ch in range(CH)]
        factors(*units[0])
        for before, unit in zip(units[:-1], units[1:]):
            factors(*unit)
            gather(*before)
        gather(*units[-1])


def first_kernel(label_ref, scale_ref, x_ref, sums, left, right):
    @pl.when(pl.program_id(0) == 0)
    def _():
        sums[...] = jnp.zeros_like(sums)

    accumulate(label_ref, scale_ref, x_ref, left, right, sums)


def last_kernel(
    label_ref,
    scale_ref,
    corner_ref,
    tile_ref,
    x_ref,
    prior_ref,
    mix_ref,
    spread_ref,
    out_ref,
    left,
    right,
    sums,
    mixed,
    wide,
    strip,
):
    tiles = out_ref.shape[0]

    @pl.when(pl.program_id(0) == 0)
    def _():
        sums[...] = prior_ref[...]

    accumulate(label_ref, scale_ref, x_ref, left, right, sums)

    @pl.when(pl.program_id(0) == pl.num_programs(0) - 1)
    def _():
        strip[...] = jnp.zeros_like(strip)
        for ch in range(CH):
            for subgrid in range(SUBW):
                mixed[ch, subgrid * 2 * SUB : (subgrid + 1) * 2 * SUB, :] = product(
                    mix_ref[...], sums[ch, subgrid], 0
                )
            wide[ch] = product(mixed[ch], spread_ref[...], 0)
            for subgrid in range(SUBW):
                shift = corner_ref[subgrid, 1]
                rows = pl.ds(corner_ref[subgrid, 0], SUB)
                top = pl.ds(subgrid * 2 * SUB, SUB)
                bottom = pl.ds(subgrid * 2 * SUB + SUB, SUB)
                real = wide[ch, top, :GCW] - wide[ch, bottom, GCW:]
                imag = wide[ch, top, GCW:] + wide[ch, bottom, :GCW]
                strip[2 * ch, rows, :] += pltpu.roll(real, shift, 1)
                strip[2 * ch + 1, rows, :] += pltpu.roll(imag, shift, 1)
        for distance in range(tiles):
            tile = lax.rem(tile_ref[0] + distance, tiles)
            rows = pl.ds(pl.multiple_of(tile * TR, TR), TR)
            for plane in range(2 * CH):
                out_ref[distance, plane] = strip[plane, rows, :]


def transform_tables():
    k = np.arange(SUB)[:, None]
    h = np.arange(HALF)[None, :]

    def tapered(x):
        return np.sin(np.pi * (x + 0.5) / SUB) ** 2 * np.exp(-2j * np.pi * k * x / SUB)

    upper, lower = tapered(HALF + h), tapered(HALF - 1 - h)
    even, odd = upper + lower, upper - lower
    table = np.concatenate([even, 1j * even, 1j * odd, -odd], axis=1)
    real, imag = table.real, table.imag
    mix = np.concatenate([real, imag], axis=0) / (ROWS * SUB)
    spread = np.zeros((TERMS, 2 * GCW))
    spread[:, :SUB] = real.T
    spread[:, GCW : GCW + SUB] = imag.T
    return mix.astype(np.float32), spread.astype(np.float32)


SUMS = (CH, SUBW, TERMS, TERMS)
ROOM = (SPAN, CH, 2, TERMS * GROUP // 2, ROWS)


def chunk_call(kernel, prefetched, arrived, extra, out_shape, scratch):
    sources = arrived.shape[0]
    whole = [pl.BlockSpec(x.shape, lambda i, *_, n=x.ndim: (0,) * n) for x in extra]
    return pl.pallas_call(
        kernel,
        out_shape=jax.ShapeDtypeStruct(out_shape, jnp.float32),
        grid_spec=pltpu.PrefetchScalarGridSpec(
            num_scalar_prefetch=len(prefetched),
            grid=(sources // SPAN,),
            in_specs=[pl.BlockSpec((SPAN, arrived.shape[1], ROWS), lambda i, *_: (i, 0, 0))]
            + whole,
            out_specs=pl.BlockSpec(out_shape, lambda i, *_: (0,) * len(out_shape)),
            scratch_shapes=[pltpu.VMEM(shape, jnp.float32) for shape in [ROOM, ROOM] + scratch],
        ),
        compiler_params=pltpu.CompilerParams(
            dimension_semantics=("arbitrary",), vmem_limit_bytes=36 << 20
        ),
        cost_estimate=pl.CostEstimate(
            flops=3 * 2 * CH * sources * GROUP * TERMS * TERMS * ROWS,
            bytes_accessed=4 * (arrived.size + math.prod(out_shape)),
            transcendentals=0,
        ),
    )(*prefetched, arrived, *extra)


def summed_around(parts, axis):
    size = lax.axis_size(axis)

    def sent(value, hops):
        return lax.ppermute(value, axis, [(i, (i + hops) % size) for i in range(size)])

    rising = sent(jnp.concatenate([parts[3], parts[4, :CH]]), 2)
    falling = sent(jnp.concatenate([parts[5], parts[4, CH:]]), -2)
    planes = 2 * CH
    pieces = [
        sent(jnp.concatenate([parts[2, :CH] + rising[planes:], parts[2, CH:]]), 2),
        sent(jnp.concatenate([parts[6, :CH], parts[6, CH:] + falling[planes:]]), -2),
        sent(parts[1] + rising[:planes], 1),
        sent(parts[7] + falling[:planes], -1),
    ]
    return sum(pieces, parts[0])


def local(block_coords, block_visibilities, subgrid_of_block, live_blocks, corners, channel_scale):
    workers = lax.axis_size("work")
    tiles = lax.axis_size("tile")
    worker = lax.axis_index("work")
    coords = jnp.swapaxes(block_coords, 0, 1)
    local_corners = lax.dynamic_slice_in_dim(corners, worker * SUBW, SUBW, 0)
    local_corners = local_corners - jnp.stack([0 * worker, worker * GCW])[None, :]
    factors = jnp.concatenate(
        [channel_scale * (2.0 * math.pi / (2 * SUB)), channel_scale * (math.pi / (SUB * SUB))]
    )
    sums = None
    for chunk in range(CHUNKS):
        packed = pack(
            chunk, subgrid_of_block, live_blocks, coords, block_visibilities, workers
        )
        arrived = lax.all_to_all(packed, "work", split_axis=0, concat_axis=0, tiled=True)
        labels = arrived[:, FIELDS * GROUP, :GROUP].astype(jnp.int32).reshape(workers * GROUP) - 1
        if chunk == 0:
            sums = chunk_call(first_kernel, (labels, factors), arrived, (), SUMS, [])
    mix, spread = transform_tables()
    tile = lax.axis_index("tile").astype(jnp.int32).reshape(1)
    parts = chunk_call(
        last_kernel,
        (labels, factors, local_corners, tile),
        arrived,
        (sums, jnp.asarray(mix), jnp.asarray(spread)),
        (tiles, 2 * CH, TR, GCW),
        [
            SUMS,
            (CH, SUBW * 2 * SUB, TERMS),
            (CH, SUBW * 2 * SUB, 2 * GCW),
            (2 * CH, TR * tiles, GCW),
        ],
    )
    return summed_around(parts, "tile")


def solution(mesh):
    return jax.shard_map(
        local,
        mesh=mesh,
        in_specs=(
            P(("work", "tile"), None, None),
            P(("work", "tile"), None, None),
            P(("work", "tile")),
            P(("work", "tile")),
            P(),
            P(),
        ),
        out_specs=P(None, "tile", "work"),
        check_vma=False,
    )
```
